32 devices in a mesh: shot: 2 (over y), gy: 4 (over z), freq: 2 (over x), fld: 2 (over core).
Axes of the slice: x: 2, y: 2, z: 4, core: 2. Of those that a mesh axis runs over, the one named last changes fastest.
Arguments:
- wavefields: float32 [2, 2, 8, 1024, 1024], P('fld', None, ('shot', 'freq'), 'gy'), parts along dimension 2, may hold values from -6 to 6
- slowness: float32 [2, 1024, 1024], P(None, 'gy'), may hold values from 0.7 to 1.3
- freq_index: int32 [4], P('freq'), may hold values from 15 to 27
Outputs:
- image: float32 [4, 1024, 1024], P('shot', 'gy', ('freq', 'fld')), parts along dimension 0
The draws below stay inside these ranges and needn't reach their ends.
There are 2 independent parts, one for each index of `shot`. The reference program is written for one: setup_inputs(seed, part) draws one part's arguments, and reference() takes and returns one part's arrays. A program takes and returns all parts, laid end to end along the dimension named above; an argument that names none is the same for every part. Nothing has to cross between parts.
Inputs may be any that keep to these rules, and one draw needn't show every extreme that they name: `freq_index`: frequency index k stands for the angular frequency 0.1 k.
All inputs are finite; a program needn't handle non-finite values.
Results may differ from the reference program's by a relative error of at most 0.0003.
Values sent between devices are 32-bit elements; how exact they have to be, the bound alone decides.
A program may use at most 64 MiB of HBM per device.

```python
import math
import jax
import jax.numpy as jnp
from jax import lax

NX = 1024
NY = 1024
DEPTH = 2
F = 4


def with_ends(array, own_key, smallest, high):
    index_at = [jax.random.randint(jax.random.fold_in(own_key, axis), (), 0, length) for axis, length in enumerate(array.shape)]
    main_axis = array.shape.index(max(array.shape))
    neighbour = index_at[:main_axis] + [(index_at[main_axis] + 1) % array.shape[main_axis]] + index_at[main_axis + 1:]
    return array.at[tuple(index_at)].set(smallest).at[tuple(neighbour)].set(high)


def steps_of(own_key, dims, cuts, smallest, top_value):
    gain = 1.0
    for position, blocks in cuts:
        steps = jax.random.uniform(jax.random.fold_in(jax.random.fold_in(own_key, 6), position), (blocks,), jnp.float32, smallest / len(cuts), top_value / len(cuts))
        gain = gain * jnp.repeat(jnp.exp(steps), dims[position] // blocks).reshape((-1,) + (1,) * (len(dims) - 1 - position))
    return gain


def centred(key, dims, deviation, most, shards=(), held_as=jnp.bfloat16):
    entries = jax.random.normal(key, dims, jnp.float32) * deviation
    if len(shards) > 0:
        entries = steps_of(key, dims, shards, -0.22, 0.18) * entries
    return jnp.clip(entries, min=-most, max=most).astype(held_as)


def setup_inputs(seed: int = 0, part: int = 0) -> dict:
    streams_of = jax.random.split(jax.random.key(seed), 4)
    part_splits = jax.random.split(jax.random.fold_in(streams_of[3], part), 4)
    wavefields = centred(part_splits[0], (2, 2, F, NX, NY), 1.0, 6.0, ((0, 2), (2, 2), (3, 4)), jnp.float32)
    slowness = jnp.clip(0.7 + 0.59999996 * jax.random.uniform(streams_of[1], (DEPTH, NX, NY), jnp.float32) ** steps_of(streams_of[1], (DEPTH, NX, NY), ((1, 4),), -0.2, 0.2), 0.7, 1.3)
    freq_index = with_ends(jax.random.randint(streams_of[2], (F,), 15, 28), jax.random.fold_in(streams_of[2], 1), 15, 27).astype(jnp.int32)
    return dict(wavefields=wavefields, slowness=slowness, freq_index=freq_index)


omega_unit = 0.1
reference_slowness = 1.0
depth_interval = 1.0

def wave_number(length):
    indices = jnp.arange(length, dtype=jnp.int32)
    signed = jnp.where(indices < length // 2, indices, indices - length)
    return 2.0 * math.pi / length * signed.astype(jnp.float32)

def one_step(wavefield, omega_now, polarity, screen, kz_square):
    spectrum = jnp.fft.fft2(wavefield)
    kz_root = jnp.sqrt(jnp.abs(kz_square))
    travels = kz_square >= 0.0
    amplitude = jnp.where(travels, 1.0, jnp.exp(-kz_root * depth_interval))
    angles = jnp.where(travels, polarity * kz_root * depth_interval, 0.0)
    spectrum = spectrum * lax.complex(amplitude * jnp.cos(angles), amplitude * jnp.sin(angles))
    wavefield = jnp.fft.ifft2(spectrum)
    phases = polarity * omega_now * (screen - reference_slowness) * depth_interval
    return wavefield * lax.complex(jnp.cos(phases), jnp.sin(phases))

def reference(wavefields, slowness, freq_index):
    x_waves = wave_number(NX)
    y_waves = wave_number(NY)
    lateral = x_waves[:, None] ** 2 + y_waves[None, :] ** 2
    stacked = jnp.moveaxis(wavefields, 2, 0)

    def accumulate(images, inputs):
        fields, freq_now = inputs
        omega_now = omega_unit * freq_now.astype(jnp.float32)
        kz_square = (omega_now * reference_slowness) ** 2 - lateral
        source = lax.complex(fields[0, 0], fields[0, 1])
        receiver = lax.complex(fields[1, 0], fields[1, 1])
        term_list = []
        for depth_step in range(DEPTH):
            source = one_step(source, omega_now, -1.0, slowness[depth_step], kz_square)
            receiver = one_step(receiver, omega_now, 1.0, slowness[depth_step], kz_square)
            term_list.append(jnp.real(source) * jnp.real(receiver) + jnp.imag(source) * jnp.imag(receiver))
        return (images + jnp.stack(term_list), None)
    images, unused = lax.scan(accumulate, jnp.zeros((DEPTH, NX, NY), jnp.float32), (stacked, freq_index))
    return images
```

```python
import functools
import math

import jax
import jax.numpy as jnp
import numpy as np
from jax import lax
from jax.experimental import pallas as pl
from jax.experimental.pallas import tpu as pltpu
from jax.sharding import PartitionSpec as P

DEPTH = 2


omega_unit = 0.1
reference_slowness = 1.0
depth_interval = 1.0
inner_length = 128


def contract(pattern, values, matrix):
    return jnp.einsum(
        pattern, values, matrix, precision=lax.Precision.HIGHEST, preferred_element_type=jnp.float32
    )


def complex_table(length, polarity):
    indices = jnp.arange(length, dtype=jnp.int32)
    angles = (
        2.0 * math.pi / length * (indices[:, None] * indices[None, :] % length).astype(jnp.float32)
    )
    cosine = jnp.cos(angles)
    sine_part = polarity * jnp.sin(angles)
    upper = jnp.stack([cosine, sine_part], axis=1)
    lower = jnp.stack([-sine_part, cosine], axis=1)
    return jnp.stack([upper, lower], axis=0)


def twiddle(outer_size, inner_size, length, polarity):
    outer_index = jnp.arange(outer_size, dtype=jnp.int32)[:, None]
    inner_index = jnp.arange(inner_size, dtype=jnp.int32)[None, :]
    angles = 2.0 * math.pi / length * (outer_index * inner_index % length).astype(jnp.float32)
    return (jnp.cos(angles), polarity * jnp.sin(angles))


def rotate(values, cosine, sine_part):
    real_part = values[0]
    imag_part = values[1]
    return jnp.stack(
        [real_part * cosine - imag_part * sine_part, real_part * sine_part + imag_part * cosine]
    )


def wave_number(indices, length):
    signed = jnp.where(indices < length // 2, indices, indices - length)
    return 2.0 * math.pi / length * signed.astype(jnp.float32)


def forward_rows(wave_field):
    batches, x_rows, y_cols = wave_field.shape[1:]
    outer_size = y_cols // inner_length
    blocks = wave_field.reshape(2, batches, x_rows, outer_size, inner_length)
    blocks = contract("cbxan,cadk->dbxkn", blocks, complex_table(outer_size, -1.0))
    cosine, sine_part = twiddle(outer_size, inner_length, y_cols, -1.0)
    blocks = rotate(blocks, cosine, sine_part)
    blocks = contract("cbxkn,cndm->dbxkm", blocks, complex_table(inner_length, -1.0))
    return blocks.reshape(2, batches, x_rows, y_cols)


def inverse_rows(wave_field):
    batches, x_rows, y_cols = wave_field.shape[1:]
    outer_size = y_cols // inner_length
    blocks = wave_field.reshape(2, batches, x_rows, outer_size, inner_length)
    blocks = contract("cbxkm,cmdn->dbxkn", blocks, complex_table(inner_length, 1.0))
    cosine, sine_part = twiddle(outer_size, inner_length, y_cols, 1.0)
    blocks = rotate(blocks, cosine, sine_part)
    blocks = contract("cbxkn,ckda->dbxan", blocks, complex_table(outer_size, 1.0))
    return blocks.reshape(2, batches, x_rows, y_cols) / y_cols


def forward_columns(blocks):
    inner_size = blocks.shape[2]
    pencils = blocks.shape[3]
    blocks = contract("cbnsy,csdk->dbnky", blocks, complex_table(pencils, -1.0))
    cosine, sine_part = twiddle(pencils, inner_size, inner_size * pencils, -1.0)
    blocks = rotate(blocks, cosine.T[:, :, None], sine_part.T[:, :, None])
    return contract("cbnky,cndm->dbmky", blocks, complex_table(inner_size, -1.0))


def inverse_columns(blocks):
    inner_size = blocks.shape[2]
    pencils = blocks.shape[3]
    blocks = contract("cbmky,cmdn->dbnky", blocks, complex_table(inner_size, 1.0))
    cosine, sine_part = twiddle(pencils, inner_size, inner_size * pencils, 1.0)
    blocks = rotate(blocks, cosine.T[:, :, None], sine_part.T[:, :, None])
    blocks = contract("cbnky,ckds->dbnsy", blocks, complex_table(pencils, 1.0))
    return blocks / (inner_size * pencils)


def propagate(blocks, omegas, polarities, y_total):
    inner_size, pencils, y_local = blocks.shape[2:]
    x_index = (
        jnp.arange(pencils, dtype=jnp.int32)[None, :]
        + pencils * jnp.arange(inner_size, dtype=jnp.int32)[:, None]
    )
    stored = lax.axis_index("gy") * y_local + jnp.arange(y_local, dtype=jnp.int32)
    y_index = stored // inner_length + y_total // inner_length * (stored % inner_length)
    x_waves = wave_number(x_index, inner_size * pencils)
    y_waves = wave_number(y_index, y_total)
    lateral = x_waves[:, :, None] ** 2 + y_waves[None, None, :] ** 2
    kz_square = ((omegas * reference_slowness) ** 2)[:, None, None, None] - lateral[None]
    kz_root = jnp.sqrt(jnp.abs(kz_square))
    travels = kz_square >= 0.0
    amplitude = jnp.where(travels, 1.0, jnp.exp(-kz_root * depth_interval))
    angles = jnp.where(travels, polarities[:, None, None, None] * kz_root * depth_interval, 0.0)
    return rotate(blocks, amplitude * jnp.cos(angles), amplitude * jnp.sin(angles))


def apply_screen(wave_field, slowness_now, omegas, polarities):
    phases = (polarities * omegas)[:, None, None] * (
        (slowness_now - reference_slowness) * depth_interval
    )[None]
    return rotate(wave_field, jnp.cos(phases), jnp.sin(phases))


def per_device(wavefields, slowness, freq_index):
    x_rows = wavefields.shape[3]
    y_cols = wavefields.shape[4]
    pencils = lax.axis_size("gy")
    freq_devs = lax.axis_size("freq")
    fld_devs = lax.axis_size("fld")
    column_width = y_cols // (freq_devs * fld_devs)
    omegas = omega_unit * freq_index.astype(jnp.float32)
    per_side = wavefields.shape[2] // fld_devs
    regrouped = wavefields.reshape(2, 1, fld_devs, per_side, x_rows, y_cols)
    paired = lax.all_to_all(regrouped, "fld", split_axis=2, concat_axis=1, tiled=True)
    wave_field = paired.reshape(2, fld_devs * per_side, x_rows, y_cols)
    local_omegas = lax.dynamic_slice_in_dim(omegas, lax.axis_index("fld") * per_side, per_side)
    omegas = jnp.tile(local_omegas, fld_devs)
    polarities = jnp.repeat(jnp.array([-1.0, 1.0], jnp.float32), per_side)
    batches = wave_field.shape[1]
    images = []
    for depth_step in range(DEPTH):
        wave_field = forward_rows(wave_field)
        blocks = wave_field.reshape(2, batches, x_rows, pencils, y_cols // pencils)
        blocks = lax.all_to_all(blocks, "gy", split_axis=3, concat_axis=3, tiled=True)
        blocks = forward_columns(blocks)
        blocks = propagate(blocks, omegas, polarities, y_cols)
        blocks = inverse_columns(blocks)
        blocks = lax.all_to_all(blocks, "gy", split_axis=3, concat_axis=3, tiled=True)
        wave_field = inverse_rows(blocks.reshape(2, batches, x_rows, y_cols))
        wave_field = apply_screen(wave_field, slowness[depth_step], omegas, polarities)
        source = wave_field[:, :per_side]
        receiver = wave_field[:, per_side:]
        summed = jnp.sum(source[0] * receiver[0] + source[1] * receiver[1], axis=0)
        partial_image = summed.reshape(x_rows, freq_devs * fld_devs, column_width)[None]
        images.append(
            lax.psum_scatter(partial_image, ("freq", "fld"), scatter_dimension=2, tiled=True)
        )
    combined = jnp.concatenate(images, axis=0)
    return combined.reshape(DEPTH, x_rows, column_width)


radix = 4
MESH = pl.DeviceIdType.MESH


def split_table(length):
    index = np.arange(length)
    angles = 2.0 * np.pi / length * (index[:, None] * index[None, :] % length)
    cosine, sine = np.cos(angles), np.sin(angles)
    right = np.block([[cosine, -sine], [sine, cosine]]).astype(np.float32)
    high = right.astype(jnp.bfloat16)
    low = (right - high.astype(np.float32)).astype(jnp.bfloat16)
    return np.stack([high, low]), np.stack([high.T, low.T])


def twiddle_angles(length):
    short = length // radix
    return 2.0 * np.pi / length * (np.arange(radix)[:, None] * np.arange(short)[None, :])


def halves(values):
    high = values.astype(jnp.bfloat16)
    return high, (values - high.astype(jnp.float32)).astype(jnp.bfloat16)


def dot32(left, right):
    return jnp.dot(left, right, preferred_element_type=jnp.float32)


def times_table(values, table):
    high, low = halves(values)
    return dot32(high, table[0]) + (dot32(low, table[0]) + dot32(high, table[1]))


def table_times(table, values):
    high, low = halves(values)
    return dot32(table[0], high) + (dot32(table[0], low) + dot32(table[1], high))


def butterfly(parts, sign):
    (r0, i0), (r1, i1), (r2, i2), (r3, i3) = parts
    ar, ai, br, bi = r0 + r2, i0 + i2, r0 - r2, i0 - i2
    cr, ci, dr, di = r1 + r3, i1 + i3, r1 - r3, i1 - i3
    er, ei = -sign * di, sign * dr
    return [(ar + cr, ai + ci), (br + er, bi + ei), (ar - cr, ai - ci), (br - er, bi - ei)]


def turn(part, cosine, sine):
    return part[0] * cosine - part[1] * sine, part[0] * sine + part[1] * cosine


def rows_forward(parts, table, twiddles):
    rows, short = parts[0][0].shape
    parts = butterfly(parts, -1.0)
    parts = [parts[0]] + [turn(parts[k], twiddles[0, k:k + 1], -twiddles[1, k:k + 1]) for k in range(1, radix)]
    stacked = jnp.concatenate([jnp.concatenate(part, axis=1) for part in parts], axis=0)
    spectra = times_table(stacked, table)
    return [(spectra[k * rows:(k + 1) * rows, :short], spectra[k * rows:(k + 1) * rows, short:]) for k in range(radix)]


def rows_inverse(parts, table, twiddles):
    rows, short = parts[0][0].shape
    stacked = jnp.concatenate([jnp.concatenate(part, axis=1) for part in parts], axis=0)
    fields = times_table(stacked, table)
    parts = [(fields[k * rows:(k + 1) * rows, :short], fields[k * rows:(k + 1) * rows, short:]) for k in range(radix)]
    parts = [parts[0]] + [turn(parts[k], twiddles[0, k:k + 1], twiddles[1, k:k + 1]) for k in range(1, radix)]
    return butterfly(parts, 1.0)


def small_sincos(angle):
    square = angle * angle
    sine = 1.0
    for n in (14, 12, 10, 8, 6, 4, 2):
        sine = 1.0 - square * (1.0 / (n * (n + 1))) * sine
    cosine = 1.0
    for n in (13, 11, 9, 7, 5, 3, 1):
        cosine = 1.0 - square * (1.0 / (n * (n + 1))) * cosine
    return angle * sine, cosine


def spread_kernel(axes, x_total, y_total, step_rows, fields_ref, scalars_ref, out_ref, prop_ref, send_sem, recv_sem, self_sem):
    gy, fld = axes
    me, core = lax.axis_index("gy"), lax.axis_index("fld")
    freqs = fields_ref.shape[2]
    half = out_ref.shape[2]
    barrier = pltpu.get_barrier_semaphore()
    for dz in range(gy):
        for dc in range(fld):
            if dz + dc > 0:
                pl.semaphore_signal(
                    barrier, inc=1, device_id_type=MESH,
                    device_id={"gy": lax.rem(me + dz, gy), "fld": lax.rem(core + dc, fld)},
                )
    pl.semaphore_wait(barrier, gy * fld - 1)

    def remote(f, h):
        return pltpu.make_async_remote_copy(
            src_ref=fields_ref.at[0, :, f, pl.ds(h * half, half), :],
            dst_ref=out_ref.at[me],
            send_sem=send_sem.at[f * fld + h],
            recv_sem=recv_sem.at[me],
            device_id={"gy": f * fld + core, "fld": h},
            device_id_type=MESH,
        )

    own_f, own_h = me // fld, core
    is_mine = lax.rem(me, fld) == core
    own = pltpu.make_async_copy(
        fields_ref.at[0, :, own_f, pl.ds(pl.multiple_of(own_h * half, half), half), :], out_ref.at[me], self_sem
    )
    order = [(f, h) for f in range(freqs) for h in range(fld)]
    for f, h in order:
        mine = jnp.logical_and(f * fld + core == me, core == h)

        @pl.when(jnp.logical_not(mine))
        def _(f=f, h=h):
            remote(f, h).start()

    @pl.when(is_mine)
    def _():
        own.start()

    omega, polarity = scalars_ref[0], scalars_ref[1]
    x_short, y_short = x_total // radix, y_total // radix
    width = prop_ref.shape[2]

    @pl.loop(0, x_total // step_rows)
    def _(step):
        start = pl.multiple_of(step * step_rows, step_rows)
        stored_x = start + lax.broadcasted_iota(jnp.int32, (step_rows, width), 0)
        stored_y = core * width + lax.broadcasted_iota(jnp.int32, (step_rows, width), 1)
        x_index = stored_x // x_short + radix * (stored_x % x_short)
        y_index = stored_y // y_short + radix * (stored_y % y_short)
        lateral = wave_number(x_index, x_total) ** 2 + wave_number(y_index, y_total) ** 2
        kz_square = (omega * reference_slowness) ** 2 - lateral
        kz_root = jnp.sqrt(jnp.abs(kz_square))
        travels = kz_square >= 0.0
        amplitude = jnp.where(travels, 1.0, jnp.exp(-kz_root * depth_interval)) * (1.0 / (x_total * y_total))
        sine, cosine = small_sincos(jnp.where(travels, 0.5 * polarity * kz_root * depth_interval, 0.0))
        prop_ref[0, pl.ds(start, step_rows), :] = amplitude * (1.0 - 2.0 * sine * sine)
        prop_ref[1, pl.ds(start, step_rows), :] = amplitude * (2.0 * sine * cosine)

    for f, h in order:
        mine = jnp.logical_and(f * fld + core == me, core == h)

        @pl.when(jnp.logical_not(mine))
        def _(f=f, h=h):
            remote(f, h).wait_send()

    for source in range(gy):
        mine = jnp.logical_and(is_mine, me == source)

        @pl.when(jnp.logical_not(mine))
        def _(source=source):
            pltpu.make_async_remote_copy(
                src_ref=out_ref.at[source], dst_ref=out_ref.at[source],
                send_sem=send_sem.at[0], recv_sem=recv_sem.at[source],
                device_id={"gy": me, "fld": 1 - core}, device_id_type=MESH,
            ).wait_recv()

    @pl.when(is_mine)
    def _():
        own.wait()


def spread(fields, scalars, gy, fld, x_total, y_total):
    half = fields.shape[3] // fld
    width = y_total // fld
    return pl.pallas_call(
        functools.partial(spread_kernel, (gy, fld), x_total, y_total, 16),
        name="spread",
        out_shape=(
            jax.ShapeDtypeStruct((gy, 2, half, y_total), jnp.float32),
            jax.ShapeDtypeStruct((2, x_total, width), jnp.float32),
        ),
        in_specs=[pl.BlockSpec(memory_space=pl.ANY), pl.BlockSpec(memory_space=pltpu.SMEM)],
        out_specs=(pl.BlockSpec(memory_space=pl.ANY), pl.BlockSpec(memory_space=pltpu.VMEM)),
        scratch_shapes=[
            pltpu.SemaphoreType.DMA((fields.shape[2] * fld,)),
            pltpu.SemaphoreType.DMA((gy,)),
            pltpu.SemaphoreType.DMA,
        ],
        compiler_params=pltpu.CompilerParams(collective_id=0, has_side_effects=True, vmem_limit_bytes=16 * 2**20),
        cost_estimate=pl.CostEstimate(flops=10**8, bytes_accessed=3 * 10**8, transcendentals=10**6),
    )(fields, scalars)


def write_spectrum(out_ref, spectra):
    per_core = radix // out_ref.shape[0]
    short = spectra[0][0].shape[1]
    for k in range(radix):
        lanes = pl.ds(k % per_core * short, short)
        for part in range(2):
            out_ref[k // per_core, 0, part, :, lanes] = spectra[k][part]


def lane_parts(ref, index, short):
    return [
        tuple(ref[index + (part, slice(None), pl.ds(n * short, short))] for part in range(2)) for n in range(radix)
    ]


def first_kernel(field_ref, table_ref, twiddle_ref, out_ref):
    short = twiddle_ref.shape[2]
    write_spectrum(out_ref, rows_forward(lane_parts(field_ref, (0,), short), table_ref, twiddle_ref[...]))


def middle_kernel(blocks_ref, prop_ref, table_ref, back_ref, twiddle_ref, out_ref):
    cores, chunks, _, half, cols = blocks_ref.shape
    short = cores * half
    parts = [
        tuple(jnp.concatenate([blocks_ref[c, n, part] for c in range(cores)], axis=0) for part in range(2))
        for n in range(chunks)
    ]
    parts = butterfly(parts, -1.0)
    fields = []
    for k in range(radix):
        cosine, sine = twiddle_ref[0, k], twiddle_ref[1, k]
        part = parts[k] if k == 0 else turn(parts[k], cosine, -sine)
        spectrum = table_times(back_ref, jnp.concatenate(part, axis=0))
        rows = slice(k * short, (k + 1) * short)
        part = turn((spectrum[:short], spectrum[short:]), prop_ref[0, rows, :], prop_ref[1, rows, :])
        field = table_times(table_ref, jnp.concatenate(part, axis=0))
        part = (field[:short], field[short:])
        fields.append(part if k == 0 else turn(part, cosine, sine))
    fields = butterfly(fields, 1.0)
    for n in range(chunks):
        for c in range(cores):
            for part in range(2):
                out_ref[c, n, part] = fields[n][part][c * half:(c + 1) * half]


def last_kernel(more, blocks_ref, slow_ref, scalars_ref, table_ref, back_ref, twiddle_ref, field_ref, *next_ref):
    short = twiddle_ref.shape[2]
    per_core = radix // blocks_ref.shape[0]
    parts = [
        tuple(blocks_ref[k // per_core, 0, part, :, pl.ds(k % per_core * short, short)] for part in range(2))
        for k in range(radix)
    ]
    parts = rows_inverse(parts, back_ref, twiddle_ref[...])
    omega, polarity = scalars_ref[0], scalars_ref[1]
    turned = []
    for n in range(radix):
        lanes = slice(n * short, (n + 1) * short)
        slow = jnp.concatenate([slow_ref[0, q, 0, :, lanes] for q in range(slow_ref.shape[1])], axis=0)
        sine, cosine = small_sincos(polarity * omega * ((slow - reference_slowness) * depth_interval))
        part = turn(parts[n], cosine, sine)
        for side in range(2):
            field_ref[0, side, :, lanes] = part[side]
        turned.append(part)
    if more:
        write_spectrum(next_ref[0], rows_forward(turned, table_ref, twiddle_ref[...]))


def one_field_per_chip(wavefields, slowness, freq_index):
    x_rows, y_total = wavefields.shape[3:]
    gy, fld = lax.axis_size("gy"), lax.axis_size("fld")
    freq_devs, shots = lax.axis_size("freq"), lax.axis_size("shot")
    x_total = x_rows * gy
    half, width = x_rows // fld, y_total // fld
    short = y_total // radix
    z, core, x = lax.axis_index("gy"), lax.axis_index("fld"), lax.axis_index("freq")
    omega = omega_unit * lax.dynamic_index_in_dim(freq_index, z // fld, keepdims=False).astype(jnp.float32)
    polarity = (2 * (z % fld) - 1).astype(jnp.float32)
    scalars = jnp.stack([omega, polarity])

    table, back = (jnp.asarray(t) for t in split_table(short))
    angles = twiddle_angles(y_total)
    lane_twiddle = jnp.asarray(np.stack([np.cos(angles), np.sin(angles)]).astype(np.float32))
    cols = min(256, width)
    row_twiddle = jnp.broadcast_to(lane_twiddle[..., None], (2, radix, short, cols))

    share = half // (freq_devs * shots)
    mine = (lax.axis_index("shot") * freq_devs + x) * share + core * half
    part_slow = lax.dynamic_slice_in_dim(slowness, mine, share, axis=1)
    slow = lax.all_gather(part_slow, ("gy", "shot", "freq"), axis=0, tiled=False)
    slow = slow.reshape(gy, freq_devs * shots, slowness.shape[0], share, y_total)

    field, prop = spread(wavefields, scalars, gy, fld, x_total, y_total)

    smem = pl.BlockSpec(memory_space=pltpu.SMEM)
    whole = pl.BlockSpec((2, 2 * short, 2 * short), lambda i: (0, 0, 0))
    lane_tw = pl.BlockSpec((2, radix, short), lambda i: (0, 0, 0))
    field_spec = pl.BlockSpec((1, 2, half, y_total), lambda i: (i, 0, 0, 0))
    spec_spec = pl.BlockSpec((fld, 1, 2, half, width), lambda i: (0, i, 0, 0, 0))
    spec_shape = jax.ShapeDtypeStruct((fld, gy, 2, half, width), jnp.float32)
    field_shape = jax.ShapeDtypeStruct((gy, 2, half, y_total), jnp.float32)
    col_spec = pl.BlockSpec((fld, gy, 2, half, cols), lambda i: (0, 0, 0, 0, i))
    params = pltpu.CompilerParams(vmem_limit_bytes=40 * 2**20)

    spectrum = pl.pallas_call(
        first_kernel, name="first", grid=(gy,), out_shape=spec_shape,
        in_specs=[field_spec, whole, lane_tw], out_specs=spec_spec, compiler_params=params,
    )(field, table, lane_twiddle)

    images = []
    for depth_step in range(DEPTH):
        more = depth_step + 1 < DEPTH
        blocks = lax.all_to_all(spectrum, "fld", split_axis=0, concat_axis=0, tiled=True)
        blocks = pl.pallas_call(
            middle_kernel, name="middle", grid=(width // cols,), out_shape=spec_shape,
            in_specs=[
                col_spec, pl.BlockSpec((2, x_total, cols), lambda i: (0, 0, i)), whole, whole,
                pl.BlockSpec((2, radix, short, cols), lambda i: (0, 0, 0, 0)),
            ],
            out_specs=col_spec, compiler_params=params,
        )(blocks, prop, table, back, row_twiddle)
        blocks = lax.all_to_all(blocks, "fld", split_axis=0, concat_axis=0, tiled=True)
        slow_spec = pl.BlockSpec(
            (1, freq_devs * shots, 1, share, y_total), lambda i, d=depth_step: (i, 0, d, 0, 0)
        )
        out = pl.pallas_call(
            functools.partial(last_kernel, more), name="last", grid=(gy,),
            out_shape=(field_shape, spec_shape) if more else (field_shape,),
            in_specs=[spec_spec, slow_spec, smem, whole, whole, lane_tw],
            out_specs=(field_spec, spec_spec) if more else (field_spec,), compiler_params=params,
        )(blocks, slow, scalars, table, back, lane_twiddle)
        if more:
            spectrum = out[1]
        images.append(image_of(out[0], z, x, gy, fld, freq_devs))
    return jnp.stack(images)


def image_of(field, z, x, gy, fld, freq_devs):
    _, _, half, y_total = field.shape
    side = z % fld
    sides = field.reshape(gy // fld, fld, 2, half, y_total)
    sent = lax.dynamic_index_in_dim(sides, 1 - side, axis=1, keepdims=False)
    kept = lax.dynamic_index_in_dim(sides, side, axis=1, keepdims=False)
    other = lax.ppermute(sent, "gy", [(i, i ^ 1) for i in range(gy)])
    term = jnp.sum(kept * other, axis=1)
    columns = term.reshape(gy // fld, half, freq_devs, y_total // freq_devs)
    sent = lax.dynamic_index_in_dim(columns, 1 - x, axis=2, keepdims=False)
    kept = lax.dynamic_index_in_dim(columns, x, axis=2, keepdims=False)
    columns = kept + lax.ppermute(sent, "freq", [(0, 1), (1, 0)])
    sent = lax.dynamic_index_in_dim(columns, 1 - z // fld, axis=0, keepdims=False)
    kept = lax.dynamic_index_in_dim(columns, z // fld, axis=0, keepdims=False)
    rows = kept + lax.ppermute(sent, "gy", [(i, i ^ 2) for i in range(gy)])
    rows = jnp.swapaxes(rows.reshape(half, fld, -1), 0, 1)
    rows = lax.all_to_all(rows, "fld", split_axis=0, concat_axis=0, tiled=True)
    return rows.reshape(half * fld, -1)


def fits(mesh, wavefields):
    shape = dict(mesh.shape)
    freqs = wavefields.shape[2] // (shape["shot"] * shape["freq"])
    x_total, y_total = wavefields.shape[3:]
    return (
        shape["gy"] == radix == freqs * shape["fld"] and shape["fld"] == 2 and shape["freq"] == 2
        and x_total == y_total and y_total % (radix * 128) == 0
        and x_total // shape["gy"] // shape["fld"] % (8 * shape["freq"] * shape["shot"]) == 0
    )


def solution(mesh):
    placed = (P("fld", None, ("shot", "freq"), "gy", None), P(None, "gy", None), P("freq"))

    def run(wavefields, slowness, freq_index):
        return jax.shard_map(
            one_field_per_chip if fits(mesh, wavefields) else per_device,
            mesh=mesh,
            in_specs=placed,
            out_specs=P("shot", "gy", ("freq", "fld")),
            check_vma=False,
        )(wavefields, slowness, freq_index)

    return run
```

```python
import functools
import math

import jax
import jax.numpy as jnp
import numpy as np
from jax import lax
from jax.experimental import pallas as pl
from jax.experimental.pallas import tpu as pltpu
from jax.sharding import PartitionSpec as P

DEPTH = 2


omega_unit = 0.1
reference_slowness = 1.0
depth_interval = 1.0
inner_length = 128


def contract(pattern, values, matrix):
    return jnp.einsum(
        pattern, values, matrix, precision=lax.Precision.HIGHEST, preferred_element_type=jnp.float32
    )


def complex_table(length, polarity):
    indices = jnp.arange(length, dtype=jnp.int32)
    angles = (
        2.0 * math.pi / length * (indices[:, None] * indices[None, :] % length).astype(jnp.float32)
    )
    cosine = jnp.cos(angles)
    sine_part = polarity * jnp.sin(angles)
    upper = jnp.stack([cosine, sine_part], axis=1)
    lower = jnp.stack([-sine_part, cosine], axis=1)
    return jnp.stack([upper, lower], axis=0)


def twiddle(outer_size, inner_size, length, polarity):
    outer_index = jnp.arange(outer_size, dtype=jnp.int32)[:, None]
    inner_index = jnp.arange(inner_size, dtype=jnp.int32)[None, :]
    angles = 2.0 * math.pi / length * (outer_index * inner_index % length).astype(jnp.float32)
    return (jnp.cos(angles), polarity * jnp.sin(angles))


def rotate(values, cosine, sine_part):
    real_part = values[0]
    imag_part = values[1]
    return jnp.stack(
        [real_part * cosine - imag_part * sine_part, real_part * sine_part + imag_part * cosine]
    )


def wave_number(indices, length):
    signed = jnp.where(indices < length // 2, indices, indices - length)
    return 2.0 * math.pi / length * signed.astype(jnp.float32)


def forward_rows(wave_field):
    batches, x_rows, y_cols = wave_field.shape[1:]
    outer_size = y_cols // inner_length
    blocks = wave_field.reshape(2, batches, x_rows, outer_size, inner_length)
    blocks = contract("cbxan,cadk->dbxkn", blocks, complex_table(outer_size, -1.0))
    cosine, sine_part = twiddle(outer_size, inner_length, y_cols, -1.0)
    blocks = rotate(blocks, cosine, sine_part)
    blocks = contract("cbxkn,cndm->dbxkm", blocks, complex_table(inner_length, -1.0))
    return blocks.reshape(2, batches, x_rows, y_cols)


def inverse_rows(wave_field):
    batches, x_rows, y_cols = wave_field.shape[1:]
    outer_size = y_cols // inner_length
    blocks = wave_field.reshape(2, batches, x_rows, outer_size, inner_length)
    blocks = contract("cbxkm,cmdn->dbxkn", blocks, complex_table(inner_length, 1.0))
    cosine, sine_part = twiddle(outer_size, inner_length, y_cols, 1.0)
    blocks = rotate(blocks, cosine, sine_part)
    blocks = contract("cbxkn,ckda->dbxan", blocks, complex_table(outer_size, 1.0))
    return blocks.reshape(2, batches, x_rows, y_cols) / y_cols


def forward_columns(blocks):
    inner_size = blocks.shape[2]
    pencils = blocks.shape[3]
    blocks = contract("cbnsy,csdk->dbnky", blocks, complex_table(pencils, -1.0))
    cosine, sine_part = twiddle(pencils, inner_size, inner_size * pencils, -1.0)
    blocks = rotate(blocks, cosine.T[:, :, None], sine_part.T[:, :, None])
    return contract("cbnky,cndm->dbmky", blocks, complex_table(inner_size, -1.0))


def inverse_columns(blocks):
    inner_size = blocks.shape[2]
    pencils = blocks.shape[3]
    blocks = contract("cbmky,cmdn->dbnky", blocks, complex_table(inner_size, 1.0))
    cosine, sine_part = twiddle(pencils, inner_size, inner_size * pencils, 1.0)
    blocks = rotate(blocks, cosine.T[:, :, None], sine_part.T[:, :, None])
    blocks = contract("cbnky,ckds->dbnsy", blocks, complex_table(pencils, 1.0))
    return blocks / (inner_size * pencils)


def propagate(blocks, omegas, polarities, y_total):
    inner_size, pencils, y_local = blocks.shape[2:]
    x_index = (
        jnp.arange(pencils, dtype=jnp.int32)[None, :]
        + pencils * jnp.arange(inner_size, dtype=jnp.int32)[:, None]
    )
    stored = lax.axis_index("gy") * y_local + jnp.arange(y_local, dtype=jnp.int32)
    y_index = stored // inner_length + y_total // inner_length * (stored % inner_length)
    x_waves = wave_number(x_index, inner_size * pencils)
    y_waves = wave_number(y_index, y_total)
    lateral = x_waves[:, :, None] ** 2 + y_waves[None, None, :] ** 2
    kz_square = ((omegas * reference_slowness) ** 2)[:, None, None, None] - lateral[None]
    kz_root = jnp.sqrt(jnp.abs(kz_square))
    travels = kz_square >= 0.0
    amplitude = jnp.where(travels, 1.0, jnp.exp(-kz_root * depth_interval))
    angles = jnp.where(travels, polarities[:, None, None, None] * kz_root * depth_interval, 0.0)
    return rotate(blocks, amplitude * jnp.cos(angles), amplitude * jnp.sin(angles))


def apply_screen(wave_field, slowness_now, omegas, polarities):
    phases = (polarities * omegas)[:, None, None] * (
        (slowness_now - reference_slowness) * depth_interval
    )[None]
    return rotate(wave_field, jnp.cos(phases), jnp.sin(phases))


def per_device(wavefields, slowness, freq_index):
    x_rows = wavefields.shape[3]
    y_cols = wavefields.shape[4]
    pencils = lax.axis_size("gy")
    freq_devs = lax.axis_size("freq")
    fld_devs = lax.axis_size("fld")
    column_width = y_cols // (freq_devs * fld_devs)
    omegas = omega_unit * freq_index.astype(jnp.float32)
    per_side = wavefields.shape[2] // fld_devs
    regrouped = wavefields.reshape(2, 1, fld_devs, per_side, x_rows, y_cols)
    paired = lax.all_to_all(regrouped, "fld", split_axis=2, concat_axis=1, tiled=True)
    wave_field = paired.reshape(2, fld_devs * per_side, x_rows, y_cols)
    local_omegas = lax.dynamic_slice_in_dim(omegas, lax.axis_index("fld") * per_side, per_side)
    omegas = jnp.tile(local_omegas, fld_devs)
    polarities = jnp.repeat(jnp.array([-1.0, 1.0], jnp.float32), per_side)
    batches = wave_field.shape[1]
    images = []
    for depth_step in range(DEPTH):
        wave_field = forward_rows(wave_field)
        blocks = wave_field.reshape(2, batches, x_rows, pencils, y_cols // pencils)
        blocks = lax.all_to_all(blocks, "gy", split_axis=3, concat_axis=3, tiled=True)
        blocks = forward_columns(blocks)
        blocks = propagate(blocks, omegas, polarities, y_cols)
        blocks = inverse_columns(blocks)
        blocks = lax.all_to_all(blocks, "gy", split_axis=3, concat_axis=3, tiled=True)
        wave_field = inverse_rows(blocks.reshape(2, batches, x_rows, y_cols))
        wave_field = apply_screen(wave_field, slowness[depth_step], omegas, polarities)
        source = wave_field[:, :per_side]
        receiver = wave_field[:, per_side:]
        summed = jnp.sum(source[0] * receiver[0] + source[1] * receiver[1], axis=0)
        partial_image = summed.reshape(x_rows, freq_devs * fld_devs, column_width)[None]
        images.append(
            lax.psum_scatter(partial_image, ("freq", "fld"), scatter_dimension=2, tiled=True)
        )
    combined = jnp.concatenate(images, axis=0)
    return combined.reshape(DEPTH, x_rows, column_width)


radix = 8
MESH = pl.DeviceIdType.MESH


def split_table(length):
    index = np.arange(length)
    angles = 2.0 * np.pi / length * (index[:, None] * index[None, :] % length)
    cosine, sine = np.cos(angles), np.sin(angles)
    right = np.block([[cosine, -sine], [sine, cosine]]).astype(np.float32)
    high = right.astype(jnp.bfloat16)
    low = (right - high.astype(np.float32)).astype(jnp.bfloat16)
    return np.stack([high, low]), np.stack([high.T, low.T])


def twiddle_angles(length):
    short = length // radix
    return 2.0 * np.pi / length * (np.arange(radix)[:, None] * np.arange(short)[None, :])


def halves(values):
    high = values.astype(jnp.bfloat16)
    return high, (values - high.astype(jnp.float32)).astype(jnp.bfloat16)


def dot32(left, right):
    return jnp.dot(left, right, preferred_element_type=jnp.float32)


def times_table(values, table):
    high, low = halves(values)
    return dot32(high, table[0]) + (dot32(low, table[0]) + dot32(high, table[1]))


def table_times(table, values):
    high, low = halves(values)
    length = table.shape[1]
    both = dot32(jnp.concatenate([table[0], table[1]], axis=0), high)
    return both[:length] + (both[length:] + dot32(table[0], low))


def butterfly(parts, sign):
    even, odd = quarter(parts[0::2], sign), quarter(parts[1::2], sign)
    root = math.sqrt(0.5)
    (_, _), (r1, i1), (r2, i2), (r3, i3) = odd
    odd = [
        odd[0],
        (root * (r1 - sign * i1), root * (i1 + sign * r1)),
        (-sign * i2, sign * r2),
        (-root * (r3 + sign * i3), root * (sign * r3 - i3)),
    ]
    added = [(e[0] + o[0], e[1] + o[1]) for e, o in zip(even, odd)]
    return added + [(e[0] - o[0], e[1] - o[1]) for e, o in zip(even, odd)]


def quarter(parts, sign):
    (r0, i0), (r1, i1), (r2, i2), (r3, i3) = parts
    ar, ai, br, bi = r0 + r2, i0 + i2, r0 - r2, i0 - i2
    cr, ci, dr, di = r1 + r3, i1 + i3, r1 - r3, i1 - i3
    er, ei = -sign * di, sign * dr
    return [(ar + cr, ai + ci), (br + er, bi + ei), (ar - cr, ai - ci), (br - er, bi - ei)]


def turn(part, cosine, sine):
    return part[0] * cosine - part[1] * sine, part[0] * sine + part[1] * cosine


def rows_forward(parts, table, twiddles):
    rows, short = parts[0][0].shape
    parts = butterfly(parts, -1.0)
    parts = [parts[0]] + [turn(parts[k], twiddles[0, k:k + 1], -twiddles[1, k:k + 1]) for k in range(1, radix)]
    stacked = jnp.concatenate([jnp.concatenate(part, axis=1) for part in parts], axis=0)
    spectra = times_table(stacked, table)
    return [(spectra[k * rows:(k + 1) * rows, :short], spectra[k * rows:(k + 1) * rows, short:]) for k in range(radix)]


def rows_inverse(parts, table, twiddles):
    rows, short = parts[0][0].shape
    stacked = jnp.concatenate([jnp.concatenate(part, axis=1) for part in parts], axis=0)
    fields = times_table(stacked, table)
    parts = [(fields[k * rows:(k + 1) * rows, :short], fields[k * rows:(k + 1) * rows, short:]) for k in range(radix)]
    parts = [parts[0]] + [turn(parts[k], twiddles[0, k:k + 1], twiddles[1, k:k + 1]) for k in range(1, radix)]
    return butterfly(parts, 1.0)


def small_sincos(angle):
    square = angle * angle
    sine = 1.0
    for n in (14, 12, 10, 8, 6, 4, 2):
        sine = 1.0 - square * (1.0 / (n * (n + 1))) * sine
    cosine = 1.0
    for n in (13, 11, 9, 7, 5, 3, 1):
        cosine = 1.0 - square * (1.0 / (n * (n + 1))) * cosine
    return angle * sine, cosine


def spread_kernel(axes, x_total, y_total, step_rows, fields_ref, scalars_ref, out_ref, prop_ref, send_sem, recv_sem, self_sem):
    gy, fld = axes
    me, core = lax.axis_index("gy"), lax.axis_index("fld")
    freqs = fields_ref.shape[2]
    half = out_ref.shape[2]
    barrier = pltpu.get_barrier_semaphore()
    for dz in range(gy):
        for dc in range(fld):
            if dz + dc > 0:
                pl.semaphore_signal(
                    barrier, inc=1, device_id_type=MESH,
                    device_id={"gy": lax.rem(me + dz, gy), "fld": lax.rem(core + dc, fld)},
                )
    pl.semaphore_wait(barrier, gy * fld - 1)

    def remote(f, h):
        return pltpu.make_async_remote_copy(
            src_ref=fields_ref.at[0, :, f, pl.ds(h * half, half), :],
            dst_ref=out_ref.at[me],
            send_sem=send_sem.at[f * fld + h],
            recv_sem=recv_sem.at[me],
            device_id={"gy": f * fld + core, "fld": h},
            device_id_type=MESH,
        )

    own_f, own_h = me // fld, core
    is_mine = lax.rem(me, fld) == core
    own = pltpu.make_async_copy(
        fields_ref.at[0, :, own_f, pl.ds(pl.multiple_of(own_h * half, half), half), :], out_ref.at[me], self_sem
    )
    order = [(f, h) for f in range(freqs) for h in range(fld)]
    for f, h in order:
        mine = jnp.logical_and(f * fld + core == me, core == h)

        @pl.when(jnp.logical_not(mine))
        def _(f=f, h=h):
            remote(f, h).start()

    @pl.when(is_mine)
    def _():
        own.start()

    omega, polarity = scalars_ref[0], scalars_ref[1]
    x_short, y_short = x_total // radix, y_total // radix
    width = prop_ref.shape[2]

    @pl.loop(0, x_total // step_rows)
    def _(step):
        start = pl.multiple_of(step * step_rows, step_rows)
        stored_x = start + lax.broadcasted_iota(jnp.int32, (step_rows, width), 0)
        stored_y = core * width + lax.broadcasted_iota(jnp.int32, (step_rows, width), 1)
        x_index = stored_x // x_short + radix * (stored_x % x_short)
        y_index = stored_y // y_short + radix * (stored_y % y_short)
        lateral = wave_number(x_index, x_total) ** 2 + wave_number(y_index, y_total) ** 2
        kz_square = (omega * reference_slowness) ** 2 - lateral
        kz_root = jnp.sqrt(jnp.abs(kz_square))
        travels = kz_square >= 0.0
        amplitude = jnp.where(travels, 1.0, jnp.exp(-kz_root * depth_interval)) * (1.0 / (x_total * y_total))
        sine, cosine = small_sincos(jnp.where(travels, 0.5 * polarity * kz_root * depth_interval, 0.0))
        prop_ref[0, pl.ds(start, step_rows), :] = amplitude * (1.0 - 2.0 * sine * sine)
        prop_ref[1, pl.ds(start, step_rows), :] = amplitude * (2.0 * sine * cosine)

    for f, h in order:
        mine = jnp.logical_and(f * fld + core == me, core == h)

        @pl.when(jnp.logical_not(mine))
        def _(f=f, h=h):
            remote(f, h).wait_send()

    for source in range(gy):
        mine = jnp.logical_and(is_mine, me == source)

        @pl.when(jnp.logical_not(mine))
        def _(source=source):
            pltpu.make_async_remote_copy(
                src_ref=out_ref.at[source], dst_ref=out_ref.at[source],
                send_sem=send_sem.at[0], recv_sem=recv_sem.at[source],
                device_id={"gy": me, "fld": 1 - core}, device_id_type=MESH,
            ).wait_recv()

    @pl.when(is_mine)
    def _():
        own.wait()


def spread(fields, scalars, gy, fld, x_total, y_total):
    half = fields.shape[3] // fld
    width = y_total // fld
    return pl.pallas_call(
        functools.partial(spread_kernel, (gy, fld), x_total, y_total, 16),
        name="spread",
        out_shape=(
            jax.ShapeDtypeStruct((gy, 2, half, y_total), jnp.float32),
            jax.ShapeDtypeStruct((2, x_total, width), jnp.float32),
        ),
        in_specs=[pl.BlockSpec(memory_space=pl.ANY), pl.BlockSpec(memory_space=pltpu.SMEM)],
        out_specs=(pl.BlockSpec(memory_space=pl.ANY), pl.BlockSpec(memory_space=pltpu.VMEM)),
        scratch_shapes=[
            pltpu.SemaphoreType.DMA((fields.shape[2] * fld,)),
            pltpu.SemaphoreType.DMA((gy,)),
            pltpu.SemaphoreType.DMA,
        ],
        compiler_params=pltpu.CompilerParams(collective_id=0, has_side_effects=True, vmem_limit_bytes=16 * 2**20),
        cost_estimate=pl.CostEstimate(flops=10**8, bytes_accessed=3 * 10**8, transcendentals=10**6),
    )(fields, scalars)


def write_spectrum(out_ref, spectra):
    per_core = radix // out_ref.shape[0]
    short = spectra[0][0].shape[1]
    for k in range(radix):
        lanes = pl.ds(k % per_core * short, short)
        for part in range(2):
            out_ref[k // per_core, 0, part, :, lanes] = spectra[k][part]


def lane_parts(ref, index, short):
    return [
        tuple(ref[index + (part, slice(None), pl.ds(n * short, short))] for part in range(2)) for n in range(radix)
    ]


def first_kernel(field_ref, table_ref, twiddle_ref, out_ref):
    short = twiddle_ref.shape[2]
    write_spectrum(out_ref, rows_forward(lane_parts(field_ref, (0,), short), table_ref, twiddle_ref[...]))


def middle_kernel(blocks_ref, prop_ref, table_ref, back_ref, twiddle_ref, out_ref):
    cores, chunks, _, short, cols = blocks_ref.shape
    parts = [(blocks_ref[c, n, 0], blocks_ref[c, n, 1]) for n in range(chunks) for c in range(cores)]
    parts = butterfly(parts, -1.0)
    fields = []
    for k in range(radix):
        cosine, sine = twiddle_ref[0, k], twiddle_ref[1, k]
        part = parts[k] if k == 0 else turn(parts[k], cosine, -sine)
        spectrum = table_times(back_ref, jnp.concatenate(part, axis=0))
        rows = slice(k * short, (k + 1) * short)
        part = turn((spectrum[:short], spectrum[short:]), prop_ref[0, rows, :], prop_ref[1, rows, :])
        field = table_times(table_ref, jnp.concatenate(part, axis=0))
        part = (field[:short], field[short:])
        fields.append(part if k == 0 else turn(part, cosine, sine))
    fields = butterfly(fields, 1.0)
    for n in range(chunks):
        for c in range(cores):
            for part in range(2):
                out_ref[c, n, part] = fields[n * cores + c][part]


def last_kernel(more, blocks_ref, slow_ref, scalars_ref, table_ref, back_ref, twiddle_ref, field_ref, *next_ref):
    short = twiddle_ref.shape[2]
    per_core = radix // blocks_ref.shape[0]
    parts = [
        tuple(blocks_ref[k // per_core, 0, part, :, pl.ds(k % per_core * short, short)] for part in range(2))
        for k in range(radix)
    ]
    parts = rows_inverse(parts, back_ref, twiddle_ref[...])
    omega, polarity = scalars_ref[0], scalars_ref[1]
    turned = []
    for n in range(radix):
        lanes = slice(n * short, (n + 1) * short)
        slow = jnp.concatenate([slow_ref[0, q, :, lanes] for q in range(slow_ref.shape[1])], axis=0)
        sine, cosine = small_sincos(polarity * omega * ((slow - reference_slowness) * depth_interval))
        part = turn(parts[n], cosine, sine)
        for side in range(2):
            field_ref[0, side, :, lanes] = part[side]
        turned.append(part)
    if more:
        write_spectrum(next_ref[0], rows_forward(turned, table_ref, twiddle_ref[...]))


def one_field_per_chip(wavefields, slowness, freq_index):
    x_rows, y_total = wavefields.shape[3:]
    gy, fld = lax.axis_size("gy"), lax.axis_size("fld")
    freq_devs, shots = lax.axis_size("freq"), lax.axis_size("shot")
    x_total = x_rows * gy
    half, width = x_rows // fld, y_total // fld
    short = y_total // radix
    z, core, x = lax.axis_index("gy"), lax.axis_index("fld"), lax.axis_index("freq")
    omega = omega_unit * lax.dynamic_index_in_dim(freq_index, z // fld, keepdims=False).astype(jnp.float32)
    polarity = (2 * (z % fld) - 1).astype(jnp.float32)
    scalars = jnp.stack([omega, polarity])

    table, back = (jnp.asarray(t) for t in split_table(short))
    angles = twiddle_angles(y_total)
    lane_twiddle = jnp.asarray(np.stack([np.cos(angles), np.sin(angles)]).astype(np.float32))
    cols = min(256, width)
    row_twiddle = jnp.broadcast_to(lane_twiddle[..., None], (2, radix, short, cols))

    share = half // (freq_devs * shots)
    mine = (lax.axis_index("shot") * freq_devs + x) * share + core * half
    part_slow = lax.dynamic_slice_in_dim(slowness, mine, share, axis=1)
    field, prop = spread(wavefields, scalars, gy, fld, x_total, y_total)
    part_slow, field = lax.optimization_barrier((part_slow, field))
    slows = [
        lax.all_gather(part_slow[d], ("gy", "shot", "freq"), axis=0, tiled=False).reshape(
            gy, freq_devs * shots, share, y_total
        )
        for d in range(DEPTH)
    ]

    smem = pl.BlockSpec(memory_space=pltpu.SMEM)
    whole = pl.BlockSpec((2, 2 * short, 2 * short), lambda i: (0, 0, 0))
    lane_tw = pl.BlockSpec((2, radix, short), lambda i: (0, 0, 0))
    field_spec = pl.BlockSpec((1, 2, half, y_total), lambda i: (i, 0, 0, 0))
    spec_spec = pl.BlockSpec((fld, 1, 2, half, width), lambda i: (0, i, 0, 0, 0))
    spec_shape = jax.ShapeDtypeStruct((fld, gy, 2, half, width), jnp.float32)
    field_shape = jax.ShapeDtypeStruct((gy, 2, half, y_total), jnp.float32)
    col_spec = pl.BlockSpec((fld, gy, 2, half, cols), lambda i: (0, 0, 0, 0, i))
    params = pltpu.CompilerParams(vmem_limit_bytes=40 * 2**20)
    cost = pl.CostEstimate(flops=12 * 2 * 2 * short * x_total * y_total // fld, bytes_accessed=12 * x_total * y_total, transcendentals=0)

    spectrum = pl.pallas_call(
        first_kernel, name="first", grid=(gy,), out_shape=spec_shape,
        in_specs=[field_spec, whole, lane_tw], out_specs=spec_spec, compiler_params=params, cost_estimate=cost,
    )(field, table, lane_twiddle)

    images = []
    for depth_step in range(DEPTH):
        more = depth_step + 1 < DEPTH
        blocks = lax.all_to_all(spectrum, "fld", split_axis=0, concat_axis=0, tiled=True)
        blocks = pl.pallas_call(
            middle_kernel, name="middle", grid=(width // cols,), out_shape=spec_shape,
            in_specs=[
                col_spec, pl.BlockSpec((2, x_total, cols), lambda i: (0, 0, i)), whole, whole,
                pl.BlockSpec((2, radix, short, cols), lambda i: (0, 0, 0, 0)),
            ],
            out_specs=col_spec, compiler_params=params, cost_estimate=cost,
        )(blocks, prop, table, back, row_twiddle)
        blocks = lax.all_to_all(blocks, "fld", split_axis=0, concat_axis=0, tiled=True)
        slow_spec = pl.BlockSpec((1, freq_devs * shots, share, y_total), lambda i: (i, 0, 0, 0))
        out = pl.pallas_call(
            functools.partial(last_kernel, more), name="last", grid=(gy,),
            out_shape=(field_shape, spec_shape) if more else (field_shape,),
            in_specs=[spec_spec, slow_spec, smem, whole, whole, lane_tw],
            out_specs=(field_spec, spec_spec) if more else (field_spec,), compiler_params=params, cost_estimate=cost,
        )(blocks, slows[depth_step], scalars, table, back, lane_twiddle)
        if more:
            spectrum = out[1]
        images.append(image_of(out[0], z, x, gy, fld, freq_devs))
    return jnp.stack(images)


def image_of(field, z, x, gy, fld, freq_devs):
    _, _, half, y_total = field.shape
    side = z % fld
    sides = field.reshape(gy // fld, fld, 2, half, y_total)
    sent = lax.dynamic_index_in_dim(sides, 1 - side, axis=1, keepdims=False)
    kept = lax.dynamic_index_in_dim(sides, side, axis=1, keepdims=False)
    other = lax.ppermute(sent, "gy", [(i, i ^ 1) for i in range(gy)])
    term = jnp.sum(kept * other, axis=1)
    columns = term.reshape(gy // fld, half, freq_devs, y_total // freq_devs)
    sent = lax.dynamic_index_in_dim(columns, 1 - x, axis=2, keepdims=False)
    kept = lax.dynamic_index_in_dim(columns, x, axis=2, keepdims=False)
    columns = kept + lax.ppermute(sent, "freq", [(0, 1), (1, 0)])
    sent = lax.dynamic_index_in_dim(columns, 1 - z // fld, axis=0, keepdims=False)
    kept = lax.dynamic_index_in_dim(columns, z // fld, axis=0, keepdims=False)
    rows = kept + lax.ppermute(sent, "gy", [(i, i ^ 2) for i in range(gy)])
    rows = jnp.swapaxes(rows.reshape(half, fld, -1), 0, 1)
    rows = lax.all_to_all(rows, "fld", split_axis=0, concat_axis=0, tiled=True)
    return rows.reshape(half * fld, -1)


def fits(mesh, wavefields):
    shape = dict(mesh.shape)
    freqs = wavefields.shape[2] // (shape["shot"] * shape["freq"])
    x_total, y_total = wavefields.shape[3:]
    return (
        shape["gy"] == 4 == freqs * shape["fld"] and shape["fld"] == 2 and shape["freq"] == 2
        and x_total == y_total and y_total % (radix * 128) == 0
        and x_total // shape["gy"] // shape["fld"] % (8 * shape["freq"] * shape["shot"]) == 0
    )


def solution(mesh):
    placed = (P("fld", None, ("shot", "freq"), "gy", None), P(None, "gy", None), P("freq"))

    def run(wavefields, slowness, freq_index):
        return jax.shard_map(
            one_field_per_chip if fits(mesh, wavefields) else per_device,
            mesh=mesh,
            in_specs=placed,
            out_specs=P("shot", "gy", ("freq", "fld")),
            check_vma=False,
        )(wavefields, slowness, freq_index)

    return run
```

```python
import functools
import math

import jax
import jax.numpy as jnp
import numpy as np
from jax import lax
from jax.experimental import pallas as pl
from jax.experimental.pallas import tpu as pltpu
from jax.sharding import PartitionSpec as P

DEPTH = 2


omega_unit = 0.1
reference_slowness = 1.0
depth_interval = 1.0
inner_length = 128


def contract(pattern, values, matrix):
    return jnp.einsum(
        pattern, values, matrix, precision=lax.Precision.HIGHEST, preferred_element_type=jnp.float32
    )


def complex_table(length, polarity):
    indices = jnp.arange(length, dtype=jnp.int32)
    angles = (
        2.0 * math.pi / length * (indices[:, None] * indices[None, :] % length).astype(jnp.float32)
    )
    cosine = jnp.cos(angles)
    sine_part = polarity * jnp.sin(angles)
    upper = jnp.stack([cosine, sine_part], axis=1)
    lower = jnp.stack([-sine_part, cosine], axis=1)
    return jnp.stack([upper, lower], axis=0)


def twiddle(outer_size, inner_size, length, polarity):
    outer_index = jnp.arange(outer_size, dtype=jnp.int32)[:, None]
    inner_index = jnp.arange(inner_size, dtype=jnp.int32)[None, :]
    angles = 2.0 * math.pi / length * (outer_index * inner_index % length).astype(jnp.float32)
    return (jnp.cos(angles), polarity * jnp.sin(angles))


def rotate(values, cosine, sine_part):
    real_part = values[0]
    imag_part = values[1]
    return jnp.stack(
        [real_part * cosine - imag_part * sine_part, real_part * sine_part + imag_part * cosine]
    )


def wave_number(indices, length):
    signed = jnp.where(indices < length // 2, indices, indices - length)
    return 2.0 * math.pi / length * signed.astype(jnp.float32)


def forward_rows(wave_field):
    batches, x_rows, y_cols = wave_field.shape[1:]
    outer_size = y_cols // inner_length
    blocks = wave_field.reshape(2, batches, x_rows, outer_size, inner_length)
    blocks = contract("cbxan,cadk->dbxkn", blocks, complex_table(outer_size, -1.0))
    cosine, sine_part = twiddle(outer_size, inner_length, y_cols, -1.0)
    blocks = rotate(blocks, cosine, sine_part)
    blocks = contract("cbxkn,cndm->dbxkm", blocks, complex_table(inner_length, -1.0))
    return blocks.reshape(2, batches, x_rows, y_cols)


def inverse_rows(wave_field):
    batches, x_rows, y_cols = wave_field.shape[1:]
    outer_size = y_cols // inner_length
    blocks = wave_field.reshape(2, batches, x_rows, outer_size, inner_length)
    blocks = contract("cbxkm,cmdn->dbxkn", blocks, complex_table(inner_length, 1.0))
    cosine, sine_part = twiddle(outer_size, inner_length, y_cols, 1.0)
    blocks = rotate(blocks, cosine, sine_part)
    blocks = contract("cbxkn,ckda->dbxan", blocks, complex_table(outer_size, 1.0))
    return blocks.reshape(2, batches, x_rows, y_cols) / y_cols


def forward_columns(blocks):
    inner_size = blocks.shape[2]
    pencils = blocks.shape[3]
    blocks = contract("cbnsy,csdk->dbnky", blocks, complex_table(pencils, -1.0))
    cosine, sine_part = twiddle(pencils, inner_size, inner_size * pencils, -1.0)
    blocks = rotate(blocks, cosine.T[:, :, None], sine_part.T[:, :, None])
    return contract("cbnky,cndm->dbmky", blocks, complex_table(inner_size, -1.0))


def inverse_columns(blocks):
    inner_size = blocks.shape[2]
    pencils = blocks.shape[3]
    blocks = contract("cbmky,cmdn->dbnky", blocks, complex_table(inner_size, 1.0))
    cosine, sine_part = twiddle(pencils, inner_size, inner_size * pencils, 1.0)
    blocks = rotate(blocks, cosine.T[:, :, None], sine_part.T[:, :, None])
    blocks = contract("cbnky,ckds->dbnsy", blocks, complex_table(pencils, 1.0))
    return blocks / (inner_size * pencils)


def propagate(blocks, omegas, polarities, y_total):
    inner_size, pencils, y_local = blocks.shape[2:]
    x_index = (
        jnp.arange(pencils, dtype=jnp.int32)[None, :]
        + pencils * jnp.arange(inner_size, dtype=jnp.int32)[:, None]
    )
    stored = lax.axis_index("gy") * y_local + jnp.arange(y_local, dtype=jnp.int32)
    y_index = stored // inner_length + y_total // inner_length * (stored % inner_length)
    x_waves = wave_number(x_index, inner_size * pencils)
    y_waves = wave_number(y_index, y_total)
    lateral = x_waves[:, :, None] ** 2 + y_waves[None, None, :] ** 2
    kz_square = ((omegas * reference_slowness) ** 2)[:, None, None, None] - lateral[None]
    kz_root = jnp.sqrt(jnp.abs(kz_square))
    travels = kz_square >= 0.0
    amplitude = jnp.where(travels, 1.0, jnp.exp(-kz_root * depth_interval))
    angles = jnp.where(travels, polarities[:, None, None, None] * kz_root * depth_interval, 0.0)
    return rotate(blocks, amplitude * jnp.cos(angles), amplitude * jnp.sin(angles))


def apply_screen(wave_field, slowness_now, omegas, polarities):
    phases = (polarities * omegas)[:, None, None] * (
        (slowness_now - reference_slowness) * depth_interval
    )[None]
    return rotate(wave_field, jnp.cos(phases), jnp.sin(phases))


def per_device(wavefields, slowness, freq_index):
    x_rows = wavefields.shape[3]
    y_cols = wavefields.shape[4]
    pencils = lax.axis_size("gy")
    freq_devs = lax.axis_size("freq")
    fld_devs = lax.axis_size("fld")
    column_width = y_cols // (freq_devs * fld_devs)
    omegas = omega_unit * freq_index.astype(jnp.float32)
    per_side = wavefields.shape[2] // fld_devs
    regrouped = wavefields.reshape(2, 1, fld_devs, per_side, x_rows, y_cols)
    paired = lax.all_to_all(regrouped, "fld", split_axis=2, concat_axis=1, tiled=True)
    wave_field = paired.reshape(2, fld_devs * per_side, x_rows, y_cols)
    local_omegas = lax.dynamic_slice_in_dim(omegas, lax.axis_index("fld") * per_side, per_side)
    omegas = jnp.tile(local_omegas, fld_devs)
    polarities = jnp.repeat(jnp.array([-1.0, 1.0], jnp.float32), per_side)
    batches = wave_field.shape[1]
    images = []
    for depth_step in range(DEPTH):
        wave_field = forward_rows(wave_field)
        blocks = wave_field.reshape(2, batches, x_rows, pencils, y_cols // pencils)
        blocks = lax.all_to_all(blocks, "gy", split_axis=3, concat_axis=3, tiled=True)
        blocks = forward_columns(blocks)
        blocks = propagate(blocks, omegas, polarities, y_cols)
        blocks = inverse_columns(blocks)
        blocks = lax.all_to_all(blocks, "gy", split_axis=3, concat_axis=3, tiled=True)
        wave_field = inverse_rows(blocks.reshape(2, batches, x_rows, y_cols))
        wave_field = apply_screen(wave_field, slowness[depth_step], omegas, polarities)
        source = wave_field[:, :per_side]
        receiver = wave_field[:, per_side:]
        summed = jnp.sum(source[0] * receiver[0] + source[1] * receiver[1], axis=0)
        partial_image = summed.reshape(x_rows, freq_devs * fld_devs, column_width)[None]
        images.append(
            lax.psum_scatter(partial_image, ("freq", "fld"), scatter_dimension=2, tiled=True)
        )
    combined = jnp.concatenate(images, axis=0)
    return combined.reshape(DEPTH, x_rows, column_width)


radix = 8
MESH = pl.DeviceIdType.MESH


def split_table(length):
    index = np.arange(length)
    angles = 2.0 * np.pi / length * (index[:, None] * index[None, :] % length)
    cosine, sine = np.cos(angles), np.sin(angles)
    right = np.block([[cosine, -sine], [sine, cosine]]).astype(np.float32)
    high = right.astype(jnp.bfloat16)
    low = (right - high.astype(np.float32)).astype(jnp.bfloat16)
    return np.stack([high, low]), np.stack([high.T, low.T])


def twiddle_angles(length):
    short = length // radix
    return 2.0 * np.pi / length * (np.arange(radix)[:, None] * np.arange(short)[None, :])


def halves(values):
    high = values.astype(jnp.bfloat16)
    return high, (values - high.astype(jnp.float32)).astype(jnp.bfloat16)


def dot32(left, right):
    return jnp.dot(left, right, preferred_element_type=jnp.float32)


def times_table(values, table):
    high, low = halves(values)
    return dot32(high, table[0]) + (dot32(low, table[0]) + dot32(high, table[1]))


def table_times(table, values):
    high, low = halves(values)
    length = table.shape[1]
    both = dot32(jnp.concatenate([table[0], table[1]], axis=0), high)
    return both[:length] + (both[length:] + dot32(table[0], low))


def butterfly(parts, sign):
    even, odd = quarter(parts[0::2], sign), quarter(parts[1::2], sign)
    root = math.sqrt(0.5)
    (_, _), (r1, i1), (r2, i2), (r3, i3) = odd
    odd = [
        odd[0],
        (root * (r1 - sign * i1), root * (i1 + sign * r1)),
        (-sign * i2, sign * r2),
        (-root * (r3 + sign * i3), root * (sign * r3 - i3)),
    ]
    added = [(e[0] + o[0], e[1] + o[1]) for e, o in zip(even, odd)]
    return added + [(e[0] - o[0], e[1] - o[1]) for e, o in zip(even, odd)]


def quarter(parts, sign):
    (r0, i0), (r1, i1), (r2, i2), (r3, i3) = parts
    ar, ai, br, bi = r0 + r2, i0 + i2, r0 - r2, i0 - i2
    cr, ci, dr, di = r1 + r3, i1 + i3, r1 - r3, i1 - i3
    er, ei = -sign * di, sign * dr
    return [(ar + cr, ai + ci), (br + er, bi + ei), (ar - cr, ai - ci), (br - er, bi - ei)]


def turn(part, cosine, sine):
    return part[0] * cosine - part[1] * sine, part[0] * sine + part[1] * cosine


def rows_forward(parts, table, twiddles):
    rows, short = parts[0][0].shape
    parts = butterfly(parts, -1.0)
    parts = [parts[0]] + [turn(parts[k], twiddles[0, k:k + 1], -twiddles[1, k:k + 1]) for k in range(1, radix)]
    stacked = jnp.concatenate([jnp.concatenate(part, axis=1) for part in parts], axis=0)
    spectra = times_table(stacked, table)
    return [(spectra[k * rows:(k + 1) * rows, :short], spectra[k * rows:(k + 1) * rows, short:]) for k in range(radix)]


def rows_inverse(parts, table, twiddles):
    rows, short = parts[0][0].shape
    stacked = jnp.concatenate([jnp.concatenate(part, axis=1) for part in parts], axis=0)
    fields = times_table(stacked, table)
    parts = [(fields[k * rows:(k + 1) * rows, :short], fields[k * rows:(k + 1) * rows, short:]) for k in range(radix)]
    parts = [parts[0]] + [turn(parts[k], twiddles[0, k:k + 1], twiddles[1, k:k + 1]) for k in range(1, radix)]
    return butterfly(parts, 1.0)


def small_sincos(angle):
    square = angle * angle
    sine = 1.0
    for n in (14, 12, 10, 8, 6, 4, 2):
        sine = 1.0 - square * (1.0 / (n * (n + 1))) * sine
    cosine = 1.0
    for n in (13, 11, 9, 7, 5, 3, 1):
        cosine = 1.0 - square * (1.0 / (n * (n + 1))) * cosine
    return angle * sine, cosine


def spread_kernel(axes, x_total, y_total, step_rows, fields_ref, slow_ref, scalars_ref, out_ref, slow_out, prop_ref,
                  send_sem, recv_sem, self_sem, near_send, near_recv, far_send, far_recv, slow_sem):
    gy, fld, freq_devs, shots = axes
    x, shot = lax.axis_index("freq"), lax.axis_index("shot")
    share = slow_out.shape[3]
    my_share = shot * freq_devs + x
    me, core = lax.axis_index("gy"), lax.axis_index("fld")
    freqs = fields_ref.shape[2]
    half = out_ref.shape[2]
    barrier = pltpu.get_barrier_semaphore()
    for dz in range(gy):
        for dc in range(fld):
            if dz + dc > 0:
                pl.semaphore_signal(
                    barrier, inc=1, device_id_type=MESH,
                    device_id={"gy": lax.rem(me + dz, gy), "fld": lax.rem(core + dc, fld)},
                )
    others = [(ds, dx) for ds in range(shots) for dx in range(freq_devs) if ds + dx > 0]

    def peer(ds, dx):
        return {"shot": lax.rem(shot + ds, shots), "freq": lax.rem(x + dx, freq_devs)}

    for ds, dx in others:
        pl.semaphore_signal(barrier, inc=1, device_id_type=MESH, device_id=peer(ds, dx))
    pl.semaphore_wait(barrier, gy * fld - 1 + len(others))

    def near(dz):
        rows = pl.ds(pl.multiple_of(core * half + my_share * share, share), share)
        return pltpu.make_async_remote_copy(
            src_ref=slow_ref.at[:, rows, :], dst_ref=slow_out.at[me, my_share],
            send_sem=near_send.at[dz - 1], recv_sem=near_recv.at[dz - 1],
            device_id={"gy": lax.rem(me + dz, gy)}, device_id_type=MESH,
        )

    def far(dz, n):
        piece = slow_out.at[lax.rem(me - dz + gy, gy), my_share]
        return pltpu.make_async_remote_copy(
            src_ref=piece, dst_ref=piece, send_sem=far_send.at[dz - 1, n], recv_sem=far_recv.at[dz - 1, n],
            device_id=peer(*others[n]), device_id_type=MESH,
        )

    def near_wait(dz):
        piece = slow_out.at[lax.rem(me - dz + gy, gy), my_share]
        pltpu.make_async_remote_copy(
            src_ref=piece, dst_ref=piece, send_sem=near_send.at[dz - 1], recv_sem=near_recv.at[dz - 1],
            device_id={"gy": lax.rem(me + dz, gy)}, device_id_type=MESH,
        ).wait_recv()

    def far_wait(dz, n):
        ds, dx = others[n]
        share_of = lax.rem(shot - ds + shots, shots) * freq_devs + lax.rem(x - dx + freq_devs, freq_devs)
        piece = slow_out.at[lax.rem(me - dz + gy, gy), share_of]
        pltpu.make_async_remote_copy(
            src_ref=piece, dst_ref=piece, send_sem=far_send.at[dz - 1, n], recv_sem=far_recv.at[dz - 1, n],
            device_id=peer(ds, dx), device_id_type=MESH,
        ).wait_recv()

    local = [
        pltpu.make_async_copy(
            slow_ref.at[:, pl.ds(pl.multiple_of(core * half + q * share, share), share), :],
            slow_out.at[me, q], slow_sem.at[q],
        )
        for q in range(freq_devs * shots)
    ]
    for dz in range(1, gy):
        near(dz).start()

    def remote(f, h):
        return pltpu.make_async_remote_copy(
            src_ref=fields_ref.at[0, :, f, pl.ds(h * half, half), :],
            dst_ref=out_ref.at[me],
            send_sem=send_sem.at[f * fld + h],
            recv_sem=recv_sem.at[me],
            device_id={"gy": f * fld + core, "fld": h},
            device_id_type=MESH,
        )

    own_f, own_h = me // fld, core
    is_mine = lax.rem(me, fld) == core
    own = pltpu.make_async_copy(
        fields_ref.at[0, :, own_f, pl.ds(pl.multiple_of(own_h * half, half), half), :], out_ref.at[me], self_sem
    )
    order = [(f, h) for f in range(freqs) for h in range(fld)]
    for f, h in order:
        mine = jnp.logical_and(f * fld + core == me, core == h)

        @pl.when(jnp.logical_not(mine))
        def _(f=f, h=h):
            remote(f, h).start()

    @pl.when(is_mine)
    def _():
        own.start()

    for copy in local:
        copy.start()

    omega, polarity = scalars_ref[0], scalars_ref[1]
    x_short, y_short = x_total // radix, y_total // radix
    width = prop_ref.shape[2]

    @pl.loop(0, x_total // step_rows)
    def _(step):
        start = pl.multiple_of(step * step_rows, step_rows)
        stored_x = start + lax.broadcasted_iota(jnp.int32, (step_rows, width), 0)
        stored_y = core * width + lax.broadcasted_iota(jnp.int32, (step_rows, width), 1)
        x_index = stored_x // x_short + radix * (stored_x % x_short)
        y_index = stored_y // y_short + radix * (stored_y % y_short)
        lateral = wave_number(x_index, x_total) ** 2 + wave_number(y_index, y_total) ** 2
        kz_square = (omega * reference_slowness) ** 2 - lateral
        kz_root = jnp.sqrt(jnp.abs(kz_square))
        travels = kz_square >= 0.0
        amplitude = jnp.where(travels, 1.0, jnp.exp(-kz_root * depth_interval)) * (1.0 / (x_total * y_total))
        sine, cosine = small_sincos(jnp.where(travels, 0.5 * polarity * kz_root * depth_interval, 0.0))
        prop_ref[0, pl.ds(start, step_rows), :] = amplitude * (1.0 - 2.0 * sine * sine)
        prop_ref[1, pl.ds(start, step_rows), :] = amplitude * (2.0 * sine * cosine)

    for dz in range(1, gy):
        near_wait(dz)
        for n in range(len(others)):
            far(dz, n).start()

    for f, h in order:
        mine = jnp.logical_and(f * fld + core == me, core == h)

        @pl.when(jnp.logical_not(mine))
        def _(f=f, h=h):
            remote(f, h).wait_send()

    for source in range(gy):
        mine = jnp.logical_and(is_mine, me == source)

        @pl.when(jnp.logical_not(mine))
        def _(source=source):
            pltpu.make_async_remote_copy(
                src_ref=out_ref.at[source], dst_ref=out_ref.at[source],
                send_sem=send_sem.at[0], recv_sem=recv_sem.at[source],
                device_id={"gy": me, "fld": 1 - core}, device_id_type=MESH,
            ).wait_recv()

    @pl.when(is_mine)
    def _():
        own.wait()

    for copy in local:
        copy.wait()
    for dz in range(1, gy):
        near(dz).wait_send()
        for n in range(len(others)):
            far_wait(dz, n)
            far(dz, n).wait_send()


def spread(fields, slowness, scalars, axes, x_total, y_total):
    gy, fld, freq_devs, shots = axes
    half = fields.shape[3] // fld
    width = y_total // fld
    return pl.pallas_call(
        functools.partial(spread_kernel, axes, x_total, y_total, 16),
        name="spread",
        out_shape=(
            jax.ShapeDtypeStruct((gy, 2, half, y_total), jnp.float32),
            jax.ShapeDtypeStruct(
                (gy, freq_devs * shots, slowness.shape[0], half // (freq_devs * shots), y_total), jnp.float32
            ),
            jax.ShapeDtypeStruct((2, x_total, width), jnp.float32),
        ),
        in_specs=[pl.BlockSpec(memory_space=pl.ANY), pl.BlockSpec(memory_space=pl.ANY), pl.BlockSpec(memory_space=pltpu.SMEM)],
        out_specs=(
            pl.BlockSpec(memory_space=pl.ANY), pl.BlockSpec(memory_space=pl.ANY), pl.BlockSpec(memory_space=pltpu.VMEM)
        ),
        scratch_shapes=[
            pltpu.SemaphoreType.DMA((fields.shape[2] * fld,)),
            pltpu.SemaphoreType.DMA((gy,)),
            pltpu.SemaphoreType.DMA,
            pltpu.SemaphoreType.DMA((gy - 1,)),
            pltpu.SemaphoreType.DMA((gy - 1,)),
            pltpu.SemaphoreType.DMA((gy - 1, freq_devs * shots - 1)),
            pltpu.SemaphoreType.DMA((gy - 1, freq_devs * shots - 1)),
            pltpu.SemaphoreType.DMA((freq_devs * shots,)),
        ],
        compiler_params=pltpu.CompilerParams(collective_id=0, has_side_effects=True, vmem_limit_bytes=16 * 2**20),
        cost_estimate=pl.CostEstimate(flops=10**8, bytes_accessed=3 * 10**8, transcendentals=10**6),
    )(fields, slowness, scalars)


def write_spectrum(out_ref, spectra):
    per_core = radix // out_ref.shape[0]
    short = spectra[0][0].shape[1]
    for k in range(radix):
        lanes = pl.ds(k % per_core * short, short)
        for part in range(2):
            out_ref[k // per_core, 0, part, :, lanes] = spectra[k][part]


def lane_parts(ref, index, short):
    return [
        tuple(ref[index + (part, slice(None), pl.ds(n * short, short))] for part in range(2)) for n in range(radix)
    ]


def first_kernel(field_ref, table_ref, twiddle_ref, out_ref):
    short = twiddle_ref.shape[2]
    write_spectrum(out_ref, rows_forward(lane_parts(field_ref, (0,), short), table_ref, twiddle_ref[...]))


def middle_kernel(blocks_ref, prop_ref, table_ref, back_ref, twiddle_ref, out_ref):
    cores, chunks, _, short, cols = blocks_ref.shape
    parts = [(blocks_ref[c, n, 0], blocks_ref[c, n, 1]) for n in range(chunks) for c in range(cores)]
    parts = butterfly(parts, -1.0)
    fields = []
    for k in range(radix):
        cosine, sine = twiddle_ref[0, k], twiddle_ref[1, k]
        part = parts[k] if k == 0 else turn(parts[k], cosine, -sine)
        spectrum = table_times(back_ref, jnp.concatenate(part, axis=0))
        rows = slice(k * short, (k + 1) * short)
        part = turn((spectrum[:short], spectrum[short:]), prop_ref[0, rows, :], prop_ref[1, rows, :])
        field = table_times(table_ref, jnp.concatenate(part, axis=0))
        part = (field[:short], field[short:])
        fields.append(part if k == 0 else turn(part, cosine, sine))
    fields = butterfly(fields, 1.0)
    for n in range(chunks):
        for c in range(cores):
            for part in range(2):
                out_ref[c, n, part] = fields[n * cores + c][part]


def last_kernel(more, blocks_ref, slow_ref, scalars_ref, table_ref, back_ref, twiddle_ref, field_ref, *next_ref):
    short = twiddle_ref.shape[2]
    per_core = radix // blocks_ref.shape[0]
    parts = [
        tuple(blocks_ref[k // per_core, 0, part, :, pl.ds(k % per_core * short, short)] for part in range(2))
        for k in range(radix)
    ]
    parts = rows_inverse(parts, back_ref, twiddle_ref[...])
    omega, polarity = scalars_ref[0], scalars_ref[1]
    turned = []
    for n in range(radix):
        lanes = slice(n * short, (n + 1) * short)
        slow = jnp.concatenate([slow_ref[0, q, 0, :, lanes] for q in range(slow_ref.shape[1])], axis=0)
        sine, cosine = small_sincos(polarity * omega * ((slow - reference_slowness) * depth_interval))
        part = turn(parts[n], cosine, sine)
        for side in range(2):
            field_ref[0, side, :, lanes] = part[side]
        turned.append(part)
    if more:
        write_spectrum(next_ref[0], rows_forward(turned, table_ref, twiddle_ref[...]))


def one_field_per_chip(wavefields, slowness, freq_index):
    x_rows, y_total = wavefields.shape[3:]
    gy, fld = lax.axis_size("gy"), lax.axis_size("fld")
    freq_devs, shots = lax.axis_size("freq"), lax.axis_size("shot")
    x_total = x_rows * gy
    half, width = x_rows // fld, y_total // fld
    short = y_total // radix
    z, core, x = lax.axis_index("gy"), lax.axis_index("fld"), lax.axis_index("freq")
    omega = omega_unit * lax.dynamic_index_in_dim(freq_index, z // fld, keepdims=False).astype(jnp.float32)
    polarity = (2 * (z % fld) - 1).astype(jnp.float32)
    scalars = jnp.stack([omega, polarity])

    table, back = (jnp.asarray(t) for t in split_table(short))
    angles = twiddle_angles(y_total)
    lane_twiddle = jnp.asarray(np.stack([np.cos(angles), np.sin(angles)]).astype(np.float32))
    cols = min(256, width)
    row_twiddle = jnp.broadcast_to(lane_twiddle[..., None], (2, radix, short, cols))

    share = half // (freq_devs * shots)
    field, slow, prop = spread(wavefields, slowness, scalars, (gy, fld, freq_devs, shots), x_total, y_total)

    smem = pl.BlockSpec(memory_space=pltpu.SMEM)
    whole = pl.BlockSpec((2, 2 * short, 2 * short), lambda i: (0, 0, 0))
    lane_tw = pl.BlockSpec((2, radix, short), lambda i: (0, 0, 0))
    field_spec = pl.BlockSpec((1, 2, half, y_total), lambda i: (i, 0, 0, 0))
    spec_spec = pl.BlockSpec((fld, 1, 2, half, width), lambda i: (0, i, 0, 0, 0))
    spec_shape = jax.ShapeDtypeStruct((fld, gy, 2, half, width), jnp.float32)
    field_shape = jax.ShapeDtypeStruct((gy, 2, half, y_total), jnp.float32)
    col_spec = pl.BlockSpec((fld, gy, 2, half, cols), lambda i: (0, 0, 0, 0, i))
    params = pltpu.CompilerParams(vmem_limit_bytes=40 * 2**20)
    cost = pl.CostEstimate(flops=12 * 2 * 2 * short * x_total * y_total // fld, bytes_accessed=12 * x_total * y_total, transcendentals=0)

    spectrum = pl.pallas_call(
        first_kernel, name="first", grid=(gy,), out_shape=spec_shape,
        in_specs=[field_spec, whole, lane_tw], out_specs=spec_spec, compiler_params=params, cost_estimate=cost,
    )(field, table, lane_twiddle)

    images = []
    for depth_step in range(DEPTH):
        more = depth_step + 1 < DEPTH
        blocks = lax.all_to_all(spectrum, "fld", split_axis=0, concat_axis=0, tiled=True)
        blocks = pl.pallas_call(
            middle_kernel, name="middle", grid=(width // cols,), out_shape=spec_shape,
            in_specs=[
                col_spec, pl.BlockSpec((2, x_total, cols), lambda i: (0, 0, i)), whole, whole,
                pl.BlockSpec((2, radix, short, cols), lambda i: (0, 0, 0, 0)),
            ],
            out_specs=col_spec, compiler_params=params, cost_estimate=cost,
        )(blocks, prop, table, back, row_twiddle)
        blocks = lax.all_to_all(blocks, "fld", split_axis=0, concat_axis=0, tiled=True)
        slow_spec = pl.BlockSpec(
            (1, freq_devs * shots, 1, share, y_total), lambda i, d=depth_step: (i, 0, d, 0, 0)
        )
        out = pl.pallas_call(
            functools.partial(last_kernel, more), name="last", grid=(gy,),
            out_shape=(field_shape, spec_shape) if more else (field_shape,),
            in_specs=[spec_spec, slow_spec, smem, whole, whole, lane_tw],
            out_specs=(field_spec, spec_spec) if more else (field_spec,), compiler_params=params, cost_estimate=cost,
        )(blocks, slow, scalars, table, back, lane_twiddle)
        if more:
            spectrum = out[1]
        images.append(image_of(out[0], z, x, gy, fld, freq_devs))
    return jnp.stack(images)


def image_of(field, z, x, gy, fld, freq_devs):
    _, _, half, y_total = field.shape
    side = z % fld
    sides = field.reshape(gy // fld, fld, 2, half, y_total)
    sent = lax.dynamic_index_in_dim(sides, 1 - side, axis=1, keepdims=False)
    kept = lax.dynamic_index_in_dim(sides, side, axis=1, keepdims=False)
    other = lax.ppermute(sent, "gy", [(i, i ^ 1) for i in range(gy)])
    term = jnp.sum(kept * other, axis=1)
    columns = term.reshape(gy // fld, half, freq_devs, y_total // freq_devs)
    sent = lax.dynamic_index_in_dim(columns, 1 - x, axis=2, keepdims=False)
    kept = lax.dynamic_index_in_dim(columns, x, axis=2, keepdims=False)
    columns = kept + lax.ppermute(sent, "freq", [(0, 1), (1, 0)])
    sent = lax.dynamic_index_in_dim(columns, 1 - z // fld, axis=0, keepdims=False)
    kept = lax.dynamic_index_in_dim(columns, z // fld, axis=0, keepdims=False)
    rows = kept + lax.ppermute(sent, "gy", [(i, i ^ 2) for i in range(gy)])
    rows = jnp.swapaxes(rows.reshape(half, fld, -1), 0, 1)
    rows = lax.all_to_all(rows, "fld", split_axis=0, concat_axis=0, tiled=True)
    return rows.reshape(half * fld, -1)


def fits(mesh, wavefields):
    shape = dict(mesh.shape)
    freqs = wavefields.shape[2] // (shape["shot"] * shape["freq"])
    x_total, y_total = wavefields.shape[3:]
    return (
        shape["gy"] == 4 == freqs * shape["fld"] and shape["fld"] == 2 and shape["freq"] == 2
        and x_total == y_total and y_total % (radix * 128) == 0
        and x_total // shape["gy"] // shape["fld"] % (8 * shape["freq"] * shape["shot"]) == 0
    )


def solution(mesh):
    placed = (P("fld", None, ("shot", "freq"), "gy", None), P(None, "gy", None), P("freq"))

    def run(wavefields, slowness, freq_index):
        return jax.shard_map(
            one_field_per_chip if fits(mesh, wavefields) else per_device,
            mesh=mesh,
            in_specs=placed,
            out_specs=P("shot", "gy", ("freq", "fld")),
            check_vma=False,
        )(wavefields, slowness, freq_index)

    return run
```

```python
import functools
import math

import jax
import jax.numpy as jnp
import numpy as np
from jax import lax
from jax.experimental import pallas as pl
from jax.experimental.pallas import tpu as pltpu
from jax.sharding import PartitionSpec as P

DEPTH = 2


omega_unit = 0.1
reference_slowness = 1.0
depth_interval = 1.0
inner_length = 128


def contract(pattern, values, matrix):
    return jnp.einsum(
        pattern, values, matrix, precision=lax.Precision.HIGHEST, preferred_element_type=jnp.float32
    )


def complex_table(length, polarity):
    indices = jnp.arange(length, dtype=jnp.int32)
    angles = (
        2.0 * math.pi / length * (indices[:, None] * indices[None, :] % length).astype(jnp.float32)
    )
    cosine = jnp.cos(angles)
    sine_part = polarity * jnp.sin(angles)
    upper = jnp.stack([cosine, sine_part], axis=1)
    lower = jnp.stack([-sine_part, cosine], axis=1)
    return jnp.stack([upper, lower], axis=0)


def twiddle(outer_size, inner_size, length, polarity):
    outer_index = jnp.arange(outer_size, dtype=jnp.int32)[:, None]
    inner_index = jnp.arange(inner_size, dtype=jnp.int32)[None, :]
    angles = 2.0 * math.pi / length * (outer_index * inner_index % length).astype(jnp.float32)
    return (jnp.cos(angles), polarity * jnp.sin(angles))


def rotate(values, cosine, sine_part):
    real_part = values[0]
    imag_part = values[1]
    return jnp.stack(
        [real_part * cosine - imag_part * sine_part, real_part * sine_part + imag_part * cosine]
    )


def wave_number(indices, length):
    signed = jnp.where(indices < length // 2, indices, indices - length)
    return 2.0 * math.pi / length * signed.astype(jnp.float32)


def forward_rows(wave_field):
    batches, x_rows, y_cols = wave_field.shape[1:]
    outer_size = y_cols // inner_length
    blocks = wave_field.reshape(2, batches, x_rows, outer_size, inner_length)
    blocks = contract("cbxan,cadk->dbxkn", blocks, complex_table(outer_size, -1.0))
    cosine, sine_part = twiddle(outer_size, inner_length, y_cols, -1.0)
    blocks = rotate(blocks, cosine, sine_part)
    blocks = contract("cbxkn,cndm->dbxkm", blocks, complex_table(inner_length, -1.0))
    return blocks.reshape(2, batches, x_rows, y_cols)


def inverse_rows(wave_field):
    batches, x_rows, y_cols = wave_field.shape[1:]
    outer_size = y_cols // inner_length
    blocks = wave_field.reshape(2, batches, x_rows, outer_size, inner_length)
    blocks = contract("cbxkm,cmdn->dbxkn", blocks, complex_table(inner_length, 1.0))
    cosine, sine_part = twiddle(outer_size, inner_length, y_cols, 1.0)
    blocks = rotate(blocks, cosine, sine_part)
    blocks = contract("cbxkn,ckda->dbxan", blocks, complex_table(outer_size, 1.0))
    return blocks.reshape(2, batches, x_rows, y_cols) / y_cols


def forward_columns(blocks):
    inner_size = blocks.shape[2]
    pencils = blocks.shape[3]
    blocks = contract("cbnsy,csdk->dbnky", blocks, complex_table(pencils, -1.0))
    cosine, sine_part = twiddle(pencils, inner_size, inner_size * pencils, -1.0)
    blocks = rotate(blocks, cosine.T[:, :, None], sine_part.T[:, :, None])
    return contract("cbnky,cndm->dbmky", blocks, complex_table(inner_size, -1.0))


def inverse_columns(blocks):
    inner_size = blocks.shape[2]
    pencils = blocks.shape[3]
    blocks = contract("cbmky,cmdn->dbnky", blocks, complex_table(inner_size, 1.0))
    cosine, sine_part = twiddle(pencils, inner_size, inner_size * pencils, 1.0)
    blocks = rotate(blocks, cosine.T[:, :, None], sine_part.T[:, :, None])
    blocks = contract("cbnky,ckds->dbnsy", blocks, complex_table(pencils, 1.0))
    return blocks / (inner_size * pencils)


def propagate(blocks, omegas, polarities, y_total):
    inner_size, pencils, y_local = blocks.shape[2:]
    x_index = (
        jnp.arange(pencils, dtype=jnp.int32)[None, :]
        + pencils * jnp.arange(inner_size, dtype=jnp.int32)[:, None]
    )
    stored = lax.axis_index("gy") * y_local + jnp.arange(y_local, dtype=jnp.int32)
    y_index = stored // inner_length + y_total // inner_length * (stored % inner_length)
    x_waves = wave_number(x_index, inner_size * pencils)
    y_waves = wave_number(y_index, y_total)
    lateral = x_waves[:, :, None] ** 2 + y_waves[None, None, :] ** 2
    kz_square = ((omegas * reference_slowness) ** 2)[:, None, None, None] - lateral[None]
    kz_root = jnp.sqrt(jnp.abs(kz_square))
    travels = kz_square >= 0.0
    amplitude = jnp.where(travels, 1.0, jnp.exp(-kz_root * depth_interval))
    angles = jnp.where(travels, polarities[:, None, None, None] * kz_root * depth_interval, 0.0)
    return rotate(blocks, amplitude * jnp.cos(angles), amplitude * jnp.sin(angles))


def apply_screen(wave_field, slowness_now, omegas, polarities):
    phases = (polarities * omegas)[:, None, None] * (
        (slowness_now - reference_slowness) * depth_interval
    )[None]
    return rotate(wave_field, jnp.cos(phases), jnp.sin(phases))


def per_device(wavefields, slowness, freq_index):
    x_rows = wavefields.shape[3]
    y_cols = wavefields.shape[4]
    pencils = lax.axis_size("gy")
    freq_devs = lax.axis_size("freq")
    fld_devs = lax.axis_size("fld")
    column_width = y_cols // (freq_devs * fld_devs)
    omegas = omega_unit * freq_index.astype(jnp.float32)
    per_side = wavefields.shape[2] // fld_devs
    regrouped = wavefields.reshape(2, 1, fld_devs, per_side, x_rows, y_cols)
    paired = lax.all_to_all(regrouped, "fld", split_axis=2, concat_axis=1, tiled=True)
    wave_field = paired.reshape(2, fld_devs * per_side, x_rows, y_cols)
    local_omegas = lax.dynamic_slice_in_dim(omegas, lax.axis_index("fld") * per_side, per_side)
    omegas = jnp.tile(local_omegas, fld_devs)
    polarities = jnp.repeat(jnp.array([-1.0, 1.0], jnp.float32), per_side)
    batches = wave_field.shape[1]
    images = []
    for depth_step in range(DEPTH):
        wave_field = forward_rows(wave_field)
        blocks = wave_field.reshape(2, batches, x_rows, pencils, y_cols // pencils)
        blocks = lax.all_to_all(blocks, "gy", split_axis=3, concat_axis=3, tiled=True)
        blocks = forward_columns(blocks)
        blocks = propagate(blocks, omegas, polarities, y_cols)
        blocks = inverse_columns(blocks)
        blocks = lax.all_to_all(blocks, "gy", split_axis=3, concat_axis=3, tiled=True)
        wave_field = inverse_rows(blocks.reshape(2, batches, x_rows, y_cols))
        wave_field = apply_screen(wave_field, slowness[depth_step], omegas, polarities)
        source = wave_field[:, :per_side]
        receiver = wave_field[:, per_side:]
        summed = jnp.sum(source[0] * receiver[0] + source[1] * receiver[1], axis=0)
        partial_image = summed.reshape(x_rows, freq_devs * fld_devs, column_width)[None]
        images.append(
            lax.psum_scatter(partial_image, ("freq", "fld"), scatter_dimension=2, tiled=True)
        )
    combined = jnp.concatenate(images, axis=0)
    return combined.reshape(DEPTH, x_rows, column_width)


radix = 8
MESH = pl.DeviceIdType.MESH


def split_table(length):
    index = np.arange(length)
    angles = 2.0 * np.pi / length * (index[:, None] * index[None, :] % length)
    cosine, sine = np.cos(angles), np.sin(angles)
    right = np.block([[cosine, -sine], [sine, cosine]]).astype(np.float32)
    high = right.astype(jnp.bfloat16)
    low = (right - high.astype(np.float32)).astype(jnp.bfloat16)
    return np.stack([high, low]), np.stack([high.T, low.T])


def twiddle_angles(length):
    short = length // radix
    return 2.0 * np.pi / length * (np.arange(radix)[:, None] * np.arange(short)[None, :])


def halves(values):
    high = values.astype(jnp.bfloat16)
    return high, (values - high.astype(jnp.float32)).astype(jnp.bfloat16)


def dot32(left, right):
    return jnp.dot(left, right, preferred_element_type=jnp.float32)


def times_table(values, table):
    high, low = halves(values)
    return dot32(high, table[0]) + (dot32(low, table[0]) + dot32(high, table[1]))


def table_times(table, values):
    high, low = halves(values)
    length = table.shape[1]
    both = dot32(jnp.concatenate([table[0], table[1]], axis=0), high)
    return both[:length] + (both[length:] + dot32(table[0], low))


def butterfly(parts, sign):
    even, odd = quarter(parts[0::2], sign), quarter(parts[1::2], sign)
    root = math.sqrt(0.5)
    (_, _), (r1, i1), (r2, i2), (r3, i3) = odd
    odd = [
        odd[0],
        (root * (r1 - sign * i1), root * (i1 + sign * r1)),
        (-sign * i2, sign * r2),
        (-root * (r3 + sign * i3), root * (sign * r3 - i3)),
    ]
    added = [(e[0] + o[0], e[1] + o[1]) for e, o in zip(even, odd)]
    return added + [(e[0] - o[0], e[1] - o[1]) for e, o in zip(even, odd)]


def quarter(parts, sign):
    (r0, i0), (r1, i1), (r2, i2), (r3, i3) = parts
    ar, ai, br, bi = r0 + r2, i0 + i2, r0 - r2, i0 - i2
    cr, ci, dr, di = r1 + r3, i1 + i3, r1 - r3, i1 - i3
    er, ei = -sign * di, sign * dr
    return [(ar + cr, ai + ci), (br + er, bi + ei), (ar - cr, ai - ci), (br - er, bi - ei)]


def turn(part, cosine, sine):
    return part[0] * cosine - part[1] * sine, part[0] * sine + part[1] * cosine


def rows_forward(parts, table, twiddles):
    rows, short = parts[0][0].shape
    parts = butterfly(parts, -1.0)
    parts = [parts[0]] + [turn(parts[k], twiddles[0, k:k + 1], -twiddles[1, k:k + 1]) for k in range(1, radix)]
    stacked = jnp.concatenate([jnp.concatenate(part, axis=1) for part in parts], axis=0)
    spectra = times_table(stacked, table)
    return [(spectra[k * rows:(k + 1) * rows, :short], spectra[k * rows:(k + 1) * rows, short:]) for k in range(radix)]


def rows_inverse(parts, table, twiddles):
    rows, short = parts[0][0].shape
    stacked = jnp.concatenate([jnp.concatenate(part, axis=1) for part in parts], axis=0)
    fields = times_table(stacked, table)
    parts = [(fields[k * rows:(k + 1) * rows, :short], fields[k * rows:(k + 1) * rows, short:]) for k in range(radix)]
    parts = [parts[0]] + [turn(parts[k], twiddles[0, k:k + 1], twiddles[1, k:k + 1]) for k in range(1, radix)]
    return butterfly(parts, 1.0)


def small_sincos(angle):
    square = angle * angle
    sine = 1.0
    for n in (14, 12, 10, 8, 6, 4, 2):
        sine = 1.0 - square * (1.0 / (n * (n + 1))) * sine
    cosine = 1.0
    for n in (13, 11, 9, 7, 5, 3, 1):
        cosine = 1.0 - square * (1.0 / (n * (n + 1))) * cosine
    return angle * sine, cosine


def spread_kernel(axes, x_total, y_total, step_rows, fields_ref, slow_ref, scalars_ref, out_ref, slow_out, prop_ref,
                  send_sem, recv_sem, self_sem, near_send, near_recv, far_send, far_recv, slow_sem):
    gy, fld, freq_devs, shots = axes
    x, shot = lax.axis_index("freq"), lax.axis_index("shot")
    share = slow_out.shape[3]
    my_share = shot * freq_devs + x
    me, core = lax.axis_index("gy"), lax.axis_index("fld")
    freqs = fields_ref.shape[2]
    half = out_ref.shape[2]
    barrier = pltpu.get_barrier_semaphore()
    for dz in range(gy):
        for dc in range(fld):
            if dz + dc > 0:
                pl.semaphore_signal(
                    barrier, inc=1, device_id_type=MESH,
                    device_id={"gy": lax.rem(me + dz, gy), "fld": lax.rem(core + dc, fld)},
                )
    others = [(ds, dx) for ds in range(shots) for dx in range(freq_devs) if ds + dx > 0]

    def peer(ds, dx):
        return {"shot": lax.rem(shot + ds, shots), "freq": lax.rem(x + dx, freq_devs)}

    for ds, dx in others:
        pl.semaphore_signal(barrier, inc=1, device_id_type=MESH, device_id=peer(ds, dx))
    pl.semaphore_wait(barrier, gy * fld - 1 + len(others))

    def near(dz):
        rows = pl.ds(pl.multiple_of(core * half + my_share * share, share), share)
        return pltpu.make_async_remote_copy(
            src_ref=slow_ref.at[:, rows, :], dst_ref=slow_out.at[me, my_share],
            send_sem=near_send.at[dz - 1], recv_sem=near_recv.at[dz - 1],
            device_id={"gy": lax.rem(me + dz, gy)}, device_id_type=MESH,
        )

    def far(dz, n):
        piece = slow_out.at[lax.rem(me - dz + gy, gy), my_share]
        return pltpu.make_async_remote_copy(
            src_ref=piece, dst_ref=piece, send_sem=far_send.at[dz - 1, n], recv_sem=far_recv.at[dz - 1, n],
            device_id=peer(*others[n]), device_id_type=MESH,
        )

    def near_wait(dz):
        piece = slow_out.at[lax.rem(me - dz + gy, gy), my_share]
        pltpu.make_async_remote_copy(
            src_ref=piece, dst_ref=piece, send_sem=near_send.at[dz - 1], recv_sem=near_recv.at[dz - 1],
            device_id={"gy": lax.rem(me + dz, gy)}, device_id_type=MESH,
        ).wait_recv()

    def far_wait(dz, n):
        ds, dx = others[n]
        share_of = lax.rem(shot - ds + shots, shots) * freq_devs + lax.rem(x - dx + freq_devs, freq_devs)
        piece = slow_out.at[lax.rem(me - dz + gy, gy), share_of]
        pltpu.make_async_remote_copy(
            src_ref=piece, dst_ref=piece, send_sem=far_send.at[dz - 1, n], recv_sem=far_recv.at[dz - 1, n],
            device_id=peer(ds, dx), device_id_type=MESH,
        ).wait_recv()

    local = [
        pltpu.make_async_copy(
            slow_ref.at[:, pl.ds(pl.multiple_of(core * half + q * share, share), share), :],
            slow_out.at[me, q], slow_sem.at[q],
        )
        for q in range(freq_devs * shots)
    ]
    for dz in range(1, gy):
        near(dz).start()

    def remote(f, h):
        return pltpu.make_async_remote_copy(
            src_ref=fields_ref.at[0, :, f, pl.ds(h * half, half), :],
            dst_ref=out_ref.at[me],
            send_sem=send_sem.at[f * fld + h],
            recv_sem=recv_sem.at[me],
            device_id={"gy": f * fld + core, "fld": h},
            device_id_type=MESH,
        )

    own_f, own_h = me // fld, core
    is_mine = lax.rem(me, fld) == core
    own = pltpu.make_async_copy(
        fields_ref.at[0, :, own_f, pl.ds(pl.multiple_of(own_h * half, half), half), :], out_ref.at[me], self_sem
    )
    order = [(f, h) for f in range(freqs) for h in range(fld)]
    for f, h in order:
        mine = jnp.logical_and(f * fld + core == me, core == h)

        @pl.when(jnp.logical_not(mine))
        def _(f=f, h=h):
            remote(f, h).start()

    @pl.when(is_mine)
    def _():
        own.start()

    for copy in local:
        copy.start()

    omega, polarity = scalars_ref[0], scalars_ref[1]
    x_short, y_short = x_total // radix, y_total // radix
    width = prop_ref.shape[2]

    @pl.loop(0, x_total // step_rows)
    def _(step):
        start = pl.multiple_of(step * step_rows, step_rows)
        stored_x = start + lax.broadcasted_iota(jnp.int32, (step_rows, width), 0)
        stored_y = core * width + lax.broadcasted_iota(jnp.int32, (step_rows, width), 1)
        x_index = stored_x // x_short + radix * (stored_x % x_short)
        y_index = stored_y // y_short + radix * (stored_y % y_short)
        lateral = wave_number(x_index, x_total) ** 2 + wave_number(y_index, y_total) ** 2
        kz_square = (omega * reference_slowness) ** 2 - lateral
        kz_root = jnp.sqrt(jnp.abs(kz_square))
        travels = kz_square >= 0.0
        amplitude = jnp.where(travels, 1.0, jnp.exp(-kz_root * depth_interval)) * (1.0 / (x_total * y_total))
        sine, cosine = small_sincos(jnp.where(travels, 0.5 * polarity * kz_root * depth_interval, 0.0))
        prop_ref[0, pl.ds(start, step_rows), :] = amplitude * (1.0 - 2.0 * sine * sine)
        prop_ref[1, pl.ds(start, step_rows), :] = amplitude * (2.0 * sine * cosine)

    for dz in range(1, gy):
        near_wait(dz)
        for n in range(len(others)):
            far(dz, n).start()

    for f, h in order:
        mine = jnp.logical_and(f * fld + core == me, core == h)

        @pl.when(jnp.logical_not(mine))
        def _(f=f, h=h):
            remote(f, h).wait_send()

    for source in range(gy):
        mine = jnp.logical_and(is_mine, me == source)

        @pl.when(jnp.logical_not(mine))
        def _(source=source):
            pltpu.make_async_remote_copy(
                src_ref=out_ref.at[source], dst_ref=out_ref.at[source],
                send_sem=send_sem.at[0], recv_sem=recv_sem.at[source],
                device_id={"gy": me, "fld": 1 - core}, device_id_type=MESH,
            ).wait_recv()

    @pl.when(is_mine)
    def _():
        own.wait()

    for copy in local:
        copy.wait()
    for dz in range(1, gy):
        near(dz).wait_send()
        for n in range(len(others)):
            far_wait(dz, n)
            far(dz, n).wait_send()


def spread(fields, slowness, scalars, axes, x_total, y_total):
    gy, fld, freq_devs, shots = axes
    half = fields.shape[3] // fld
    width = y_total // fld
    return pl.pallas_call(
        functools.partial(spread_kernel, axes, x_total, y_total, 16),
        name="spread",
        out_shape=(
            jax.ShapeDtypeStruct((gy, 2, half, y_total), jnp.float32),
            jax.ShapeDtypeStruct(
                (gy, freq_devs * shots, slowness.shape[0], half // (freq_devs * shots), y_total), jnp.float32
            ),
            jax.ShapeDtypeStruct((2, x_total, width), jnp.float32),
        ),
        in_specs=[pl.BlockSpec(memory_space=pl.ANY), pl.BlockSpec(memory_space=pl.ANY), pl.BlockSpec(memory_space=pltpu.SMEM)],
        out_specs=(
            pl.BlockSpec(memory_space=pl.ANY), pl.BlockSpec(memory_space=pl.ANY), pl.BlockSpec(memory_space=pltpu.VMEM)
        ),
        scratch_shapes=[
            pltpu.SemaphoreType.DMA((fields.shape[2] * fld,)),
            pltpu.SemaphoreType.DMA((gy,)),
            pltpu.SemaphoreType.DMA,
            pltpu.SemaphoreType.DMA((gy - 1,)),
            pltpu.SemaphoreType.DMA((gy - 1,)),
            pltpu.SemaphoreType.DMA((gy - 1, freq_devs * shots - 1)),
            pltpu.SemaphoreType.DMA((gy - 1, freq_devs * shots - 1)),
            pltpu.SemaphoreType.DMA((freq_devs * shots,)),
        ],
        compiler_params=pltpu.CompilerParams(collective_id=0, has_side_effects=True, vmem_limit_bytes=16 * 2**20),
        cost_estimate=pl.CostEstimate(flops=10**8, bytes_accessed=3 * 10**8, transcendentals=10**6),
    )(fields, slowness, scalars)


def write_spectrum(out_ref, spectra):
    per_core = radix // out_ref.shape[0]
    short = spectra[0][0].shape[1]
    for k in range(radix):
        lanes = pl.ds(k % per_core * short, short)
        for part in range(2):
            out_ref[k // per_core, 0, part, :, lanes] = spectra[k][part]


def lane_parts(ref, index, short):
    return [
        tuple(ref[index + (part, slice(None), pl.ds(n * short, short))] for part in range(2)) for n in range(radix)
    ]


def first_kernel(field_ref, table_ref, twiddle_ref, out_ref):
    short = twiddle_ref.shape[2]
    write_spectrum(out_ref, rows_forward(lane_parts(field_ref, (0,), short), table_ref, twiddle_ref[...]))


def middle_kernel(blocks_ref, prop_ref, table_ref, back_ref, twiddle_ref, out_ref):
    cores, chunks, _, short, _ = blocks_ref.shape
    parts = [(blocks_ref[c, n, 0], blocks_ref[c, n, 1]) for n in range(chunks) for c in range(cores)]
    parts = butterfly(parts, -1.0)
    fields = []
    for k in range(radix):
        cosine, sine = twiddle_ref[0, k], twiddle_ref[1, k]
        part = parts[k] if k == 0 else turn(parts[k], cosine, -sine)
        spectrum = table_times(back_ref, jnp.concatenate(part, axis=0))
        rows = slice(k * short, (k + 1) * short)
        part = turn((spectrum[:short], spectrum[short:]), prop_ref[0, rows, :], prop_ref[1, rows, :])
        field = table_times(table_ref, jnp.concatenate(part, axis=0))
        part = (field[:short], field[short:])
        fields.append(part if k == 0 else turn(part, cosine, sine))
    fields = butterfly(fields, 1.0)
    for n in range(chunks):
        for c in range(cores):
            for part in range(2):
                out_ref[c, n, part] = fields[n * cores + c][part]


def last_kernel(more, blocks_ref, slow_ref, scalars_ref, table_ref, back_ref, twiddle_ref, field_ref, *next_ref):
    short = twiddle_ref.shape[2]
    per_core = radix // blocks_ref.shape[0]
    parts = [
        tuple(blocks_ref[k // per_core, 0, part, :, pl.ds(k % per_core * short, short)] for part in range(2))
        for k in range(radix)
    ]
    parts = rows_inverse(parts, back_ref, twiddle_ref[...])
    omega, polarity = scalars_ref[0], scalars_ref[1]
    turned = []
    for n in range(radix):
        lanes = slice(n * short, (n + 1) * short)
        slow = jnp.concatenate([slow_ref[0, q, 0, :, lanes] for q in range(slow_ref.shape[1])], axis=0)
        sine, cosine = small_sincos(polarity * omega * ((slow - reference_slowness) * depth_interval))
        part = turn(parts[n], cosine, sine)
        for side in range(2):
            field_ref[0, side, :, lanes] = part[side]
        turned.append(part)
    if more:
        write_spectrum(next_ref[0], rows_forward(turned, table_ref, twiddle_ref[...]))


def one_field_per_chip(wavefields, slowness, freq_index):
    x_rows, y_total = wavefields.shape[3:]
    gy, fld = lax.axis_size("gy"), lax.axis_size("fld")
    freq_devs, shots = lax.axis_size("freq"), lax.axis_size("shot")
    x_total = x_rows * gy
    half, width = x_rows // fld, y_total // fld
    short = y_total // radix
    z, x = lax.axis_index("gy"), lax.axis_index("freq")
    omega = omega_unit * lax.dynamic_index_in_dim(freq_index, z // fld, keepdims=False).astype(jnp.float32)
    polarity = (2 * (z % fld) - 1).astype(jnp.float32)
    scalars = jnp.stack([omega, polarity])

    table, back = (jnp.asarray(t) for t in split_table(short))
    angles = twiddle_angles(y_total)
    lane_twiddle = jnp.asarray(np.stack([np.cos(angles), np.sin(angles)]).astype(np.float32))
    cols = min(256, width)
    row_twiddle = jnp.broadcast_to(lane_twiddle[..., None], (2, radix, short, cols))

    share = half // (freq_devs * shots)
    field, slow, prop = spread(wavefields, slowness, scalars, (gy, fld, freq_devs, shots), x_total, y_total)

    smem = pl.BlockSpec(memory_space=pltpu.SMEM)
    whole = pl.BlockSpec((2, 2 * short, 2 * short), lambda i: (0, 0, 0))
    lane_tw = pl.BlockSpec((2, radix, short), lambda i: (0, 0, 0))
    field_spec = pl.BlockSpec((1, 2, half, y_total), lambda i: (i, 0, 0, 0))
    spec_spec = pl.BlockSpec((fld, 1, 2, half, width), lambda i: (0, i, 0, 0, 0))
    spec_shape = jax.ShapeDtypeStruct((fld, gy, 2, half, width), jnp.float32)
    field_shape = jax.ShapeDtypeStruct((gy, 2, half, y_total), jnp.float32)
    col_spec = pl.BlockSpec((fld, gy, 2, half, cols), lambda i: (0, 0, 0, 0, i))
    params = pltpu.CompilerParams(vmem_limit_bytes=40 * 2**20)
    cost = pl.CostEstimate(flops=12 * 2 * 2 * short * x_total * y_total // fld, bytes_accessed=12 * x_total * y_total, transcendentals=0)

    spectrum = pl.pallas_call(
        first_kernel, name="first", grid=(gy,), out_shape=spec_shape,
        in_specs=[field_spec, whole, lane_tw], out_specs=spec_spec, compiler_params=params, cost_estimate=cost,
    )(field, table, lane_twiddle)

    images = []
    for depth_step in range(DEPTH):
        more = depth_step + 1 < DEPTH
        blocks = lax.all_to_all(spectrum, "fld", split_axis=0, concat_axis=0, tiled=True)
        middle = pl.pallas_call(
            middle_kernel, name="middle", grid=(width // cols,), out_shape=spec_shape,
            in_specs=[
                col_spec, pl.BlockSpec((2, x_total, cols), lambda i: (0, 0, i)), whole, whole,
                pl.BlockSpec((2, radix, short, cols), lambda i: (0, 0, 0, 0)),
            ],
            out_specs=col_spec, compiler_params=params, cost_estimate=cost,
        )
        blocks = middle(blocks, prop, table, back, row_twiddle)
        blocks = lax.all_to_all(blocks, "fld", split_axis=0, concat_axis=0, tiled=True)
        slow_spec = pl.BlockSpec(
            (1, freq_devs * shots, 1, share, y_total), lambda i, d=depth_step: (i, 0, d, 0, 0)
        )
        out = pl.pallas_call(
            functools.partial(last_kernel, more), name="last", grid=(gy,),
            out_shape=(field_shape, spec_shape) if more else (field_shape,),
            in_specs=[spec_spec, slow_spec, smem, whole, whole, lane_tw],
            out_specs=(field_spec, spec_spec) if more else (field_spec,), compiler_params=params, cost_estimate=cost,
        )(blocks, slow, scalars, table, back, lane_twiddle)
        if more:
            spectrum = out[1]
        images.append(image_of(out[0], z, x, gy, fld, freq_devs))
    return jnp.stack(images)


def image_of(field, z, x, gy, fld, freq_devs):
    _, _, half, y_total = field.shape
    side = z % fld
    sides = field.reshape(gy // fld, fld, 2, half, y_total)
    sent = lax.dynamic_index_in_dim(sides, 1 - side, axis=1, keepdims=False)
    kept = lax.dynamic_index_in_dim(sides, side, axis=1, keepdims=False)
    other = lax.ppermute(sent, "gy", [(i, i ^ 1) for i in range(gy)])
    width = y_total // freq_devs
    term = jnp.sum(kept * other, axis=1)
    sent = lax.dynamic_slice_in_dim(term, (1 - x) * width, width, axis=2)
    kept = lax.dynamic_slice_in_dim(term, x * width, width, axis=2)
    columns = kept + lax.ppermute(sent, "freq", [(0, 1), (1, 0)])
    sent = lax.dynamic_index_in_dim(columns, 1 - z // fld, axis=0, keepdims=False)
    kept = lax.dynamic_index_in_dim(columns, z // fld, axis=0, keepdims=False)
    rows = kept + lax.ppermute(sent, "gy", [(i, i ^ 2) for i in range(gy)])
    core, width = lax.axis_index("fld"), width // fld
    sent = lax.dynamic_slice_in_dim(rows, (1 - core) * width, width, axis=1)
    kept = lax.dynamic_slice_in_dim(rows, core * width, width, axis=1)
    other = lax.ppermute(sent, "fld", [(0, 1), (1, 0)])
    first = core == 0
    return jnp.concatenate([jnp.where(first, kept, other), jnp.where(first, other, kept)], axis=0)


def fits(mesh, wavefields):
    shape = dict(mesh.shape)
    freqs = wavefields.shape[2] // (shape["shot"] * shape["freq"])
    x_total, y_total = wavefields.shape[3:]
    return (
        shape["gy"] == 4 == freqs * shape["fld"] and shape["fld"] == 2 and shape["freq"] == 2
        and x_total == y_total and y_total % (radix * 128) == 0
        and x_total // shape["gy"] // shape["fld"] % (8 * shape["freq"] * shape["shot"]) == 0
    )


def solution(mesh):
    placed = (P("fld", None, ("shot", "freq"), "gy", None), P(None, "gy", None), P("freq"))

    def run(wavefields, slowness, freq_index):
        engaged = fits(mesh, wavefields)
        step = jax.shard_map(
            one_field_per_chip if engaged else per_device,
            mesh=mesh,
            in_specs=placed,
            out_specs=P("shot", "gy", ("freq", "fld")),
            check_vma=False,
        )
        return step(wavefields, slowness, freq_index)

    return run
```

```python
import functools
import math

import jax
import jax.numpy as jnp
import numpy as np
from jax import lax
from jax.experimental import pallas as pl
from jax.experimental.pallas import tpu as pltpu
from jax.sharding import PartitionSpec as P

DEPTH = 2


omega_unit = 0.1
reference_slowness = 1.0
depth_interval = 1.0
inner_length = 128


def contract(pattern, values, matrix):
    return jnp.einsum(
        pattern, values, matrix, precision=lax.Precision.HIGHEST, preferred_element_type=jnp.float32
    )


def complex_table(length, polarity):
    indices = jnp.arange(length, dtype=jnp.int32)
    angles = (
        2.0 * math.pi / length * (indices[:, None] * indices[None, :] % length).astype(jnp.float32)
    )
    cosine = jnp.cos(angles)
    sine_part = polarity * jnp.sin(angles)
    upper = jnp.stack([cosine, sine_part], axis=1)
    lower = jnp.stack([-sine_part, cosine], axis=1)
    return jnp.stack([upper, lower], axis=0)


def twiddle(outer_size, inner_size, length, polarity):
    outer_index = jnp.arange(outer_size, dtype=jnp.int32)[:, None]
    inner_index = jnp.arange(inner_size, dtype=jnp.int32)[None, :]
    angles = 2.0 * math.pi / length * (outer_index * inner_index % length).astype(jnp.float32)
    return (jnp.cos(angles), polarity * jnp.sin(angles))


def rotate(values, cosine, sine_part):
    real_part = values[0]
    imag_part = values[1]
    return jnp.stack(
        [real_part * cosine - imag_part * sine_part, real_part * sine_part + imag_part * cosine]
    )


def wave_number(indices, length):
    signed = jnp.where(indices < length // 2, indices, indices - length)
    return 2.0 * math.pi / length * signed.astype(jnp.float32)


def forward_rows(wave_field):
    batches, x_rows, y_cols = wave_field.shape[1:]
    outer_size = y_cols // inner_length
    blocks = wave_field.reshape(2, batches, x_rows, outer_size, inner_length)
    blocks = contract("cbxan,cadk->dbxkn", blocks, complex_table(outer_size, -1.0))
    cosine, sine_part = twiddle(outer_size, inner_length, y_cols, -1.0)
    blocks = rotate(blocks, cosine, sine_part)
    blocks = contract("cbxkn,cndm->dbxkm", blocks, complex_table(inner_length, -1.0))
    return blocks.reshape(2, batches, x_rows, y_cols)


def inverse_rows(wave_field):
    batches, x_rows, y_cols = wave_field.shape[1:]
    outer_size = y_cols // inner_length
    blocks = wave_field.reshape(2, batches, x_rows, outer_size, inner_length)
    blocks = contract("cbxkm,cmdn->dbxkn", blocks, complex_table(inner_length, 1.0))
    cosine, sine_part = twiddle(outer_size, inner_length, y_cols, 1.0)
    blocks = rotate(blocks, cosine, sine_part)
    blocks = contract("cbxkn,ckda->dbxan", blocks, complex_table(outer_size, 1.0))
    return blocks.reshape(2, batches, x_rows, y_cols) / y_cols


def forward_columns(blocks):
    inner_size = blocks.shape[2]
    pencils = blocks.shape[3]
    blocks = contract("cbnsy,csdk->dbnky", blocks, complex_table(pencils, -1.0))
    cosine, sine_part = twiddle(pencils, inner_size, inner_size * pencils, -1.0)
    blocks = rotate(blocks, cosine.T[:, :, None], sine_part.T[:, :, None])
    return contract("cbnky,cndm->dbmky", blocks, complex_table(inner_size, -1.0))


def inverse_columns(blocks):
    inner_size = blocks.shape[2]
    pencils = blocks.shape[3]
    blocks = contract("cbmky,cmdn->dbnky", blocks, complex_table(inner_size, 1.0))
    cosine, sine_part = twiddle(pencils, inner_size, inner_size * pencils, 1.0)
    blocks = rotate(blocks, cosine.T[:, :, None], sine_part.T[:, :, None])
    blocks = contract("cbnky,ckds->dbnsy", blocks, complex_table(pencils, 1.0))
    return blocks / (inner_size * pencils)


def propagate(blocks, omegas, polarities, y_total):
    inner_size, pencils, y_local = blocks.shape[2:]
    x_index = (
        jnp.arange(pencils, dtype=jnp.int32)[None, :]
        + pencils * jnp.arange(inner_size, dtype=jnp.int32)[:, None]
    )
    stored = lax.axis_index("gy") * y_local + jnp.arange(y_local, dtype=jnp.int32)
    y_index = stored // inner_length + y_total // inner_length * (stored % inner_length)
    x_waves = wave_number(x_index, inner_size * pencils)
    y_waves = wave_number(y_index, y_total)
    lateral = x_waves[:, :, None] ** 2 + y_waves[None, None, :] ** 2
    kz_square = ((omegas * reference_slowness) ** 2)[:, None, None, None] - lateral[None]
    kz_root = jnp.sqrt(jnp.abs(kz_square))
    travels = kz_square >= 0.0
    amplitude = jnp.where(travels, 1.0, jnp.exp(-kz_root * depth_interval))
    angles = jnp.where(travels, polarities[:, None, None, None] * kz_root * depth_interval, 0.0)
    return rotate(blocks, amplitude * jnp.cos(angles), amplitude * jnp.sin(angles))


def apply_screen(wave_field, slowness_now, omegas, polarities):
    phases = (polarities * omegas)[:, None, None] * (
        (slowness_now - reference_slowness) * depth_interval
    )[None]
    return rotate(wave_field, jnp.cos(phases), jnp.sin(phases))


def per_device(wavefields, slowness, freq_index):
    x_rows = wavefields.shape[3]
    y_cols = wavefields.shape[4]
    pencils = lax.axis_size("gy")
    freq_devs = lax.axis_size("freq")
    fld_devs = lax.axis_size("fld")
    column_width = y_cols // (freq_devs * fld_devs)
    omegas = omega_unit * freq_index.astype(jnp.float32)
    per_side = wavefields.shape[2] // fld_devs
    regrouped = wavefields.reshape(2, 1, fld_devs, per_side, x_rows, y_cols)
    paired = lax.all_to_all(regrouped, "fld", split_axis=2, concat_axis=1, tiled=True)
    wave_field = paired.reshape(2, fld_devs * per_side, x_rows, y_cols)
    local_omegas = lax.dynamic_slice_in_dim(omegas, lax.axis_index("fld") * per_side, per_side)
    omegas = jnp.tile(local_omegas, fld_devs)
    polarities = jnp.repeat(jnp.array([-1.0, 1.0], jnp.float32), per_side)
    batches = wave_field.shape[1]
    images = []
    for depth_step in range(DEPTH):
        wave_field = forward_rows(wave_field)
        blocks = wave_field.reshape(2, batches, x_rows, pencils, y_cols // pencils)
        blocks = lax.all_to_all(blocks, "gy", split_axis=3, concat_axis=3, tiled=True)
        blocks = forward_columns(blocks)
        blocks = propagate(blocks, omegas, polarities, y_cols)
        blocks = inverse_columns(blocks)
        blocks = lax.all_to_all(blocks, "gy", split_axis=3, concat_axis=3, tiled=True)
        wave_field = inverse_rows(blocks.reshape(2, batches, x_rows, y_cols))
        wave_field = apply_screen(wave_field, slowness[depth_step], omegas, polarities)
        source = wave_field[:, :per_side]
        receiver = wave_field[:, per_side:]
        summed = jnp.sum(source[0] * receiver[0] + source[1] * receiver[1], axis=0)
        partial_image = summed.reshape(x_rows, freq_devs * fld_devs, column_width)[None]
        images.append(
            lax.psum_scatter(partial_image, ("freq", "fld"), scatter_dimension=2, tiled=True)
        )
    combined = jnp.concatenate(images, axis=0)
    return combined.reshape(DEPTH, x_rows, column_width)


radix = 8
MESH = pl.DeviceIdType.MESH


def split_table(length):
    index = np.arange(length)
    angles = 2.0 * np.pi / length * (index[:, None] * index[None, :] % length)
    cosine, sine = np.cos(angles), np.sin(angles)
    right = np.block([[cosine, -sine], [sine, cosine]]).astype(np.float32)
    high = right.astype(jnp.bfloat16)
    low = (right - high.astype(np.float32)).astype(jnp.bfloat16)
    return np.stack([high, low]), np.stack([high.T, low.T])


def twiddle_angles(length):
    short = length // radix
    return 2.0 * np.pi / length * (np.arange(radix)[:, None] * np.arange(short)[None, :])


def halves(values):
    high = values.astype(jnp.bfloat16)
    return high, (values - high.astype(jnp.float32)).astype(jnp.bfloat16)


def dot32(left, right):
    return jnp.dot(left, right, preferred_element_type=jnp.float32)


def times_table(values, table):
    high, low = halves(values)
    return dot32(high, table[0]) + (dot32(low, table[0]) + dot32(high, table[1]))


def table_times(table, values):
    high, low = halves(values)
    length = table.shape[1]
    both = dot32(jnp.concatenate([table[0], table[1]], axis=0), high)
    return both[:length] + (both[length:] + dot32(table[0], low))


def butterfly(parts, sign):
    even, odd = quarter(parts[0::2], sign), quarter(parts[1::2], sign)
    root = math.sqrt(0.5)
    (_, _), (r1, i1), (r2, i2), (r3, i3) = odd
    odd = [
        odd[0],
        (root * (r1 - sign * i1), root * (i1 + sign * r1)),
        (-sign * i2, sign * r2),
        (-root * (r3 + sign * i3), root * (sign * r3 - i3)),
    ]
    added = [(e[0] + o[0], e[1] + o[1]) for e, o in zip(even, odd)]
    return added + [(e[0] - o[0], e[1] - o[1]) for e, o in zip(even, odd)]


def quarter(parts, sign):
    (r0, i0), (r1, i1), (r2, i2), (r3, i3) = parts
    ar, ai, br, bi = r0 + r2, i0 + i2, r0 - r2, i0 - i2
    cr, ci, dr, di = r1 + r3, i1 + i3, r1 - r3, i1 - i3
    er, ei = -sign * di, sign * dr
    return [(ar + cr, ai + ci), (br + er, bi + ei), (ar - cr, ai - ci), (br - er, bi - ei)]


def turn(part, cosine, sine):
    return part[0] * cosine - part[1] * sine, part[0] * sine + part[1] * cosine


def rows_forward(parts, table, twiddles):
    rows, short = parts[0][0].shape
    parts = butterfly(parts, -1.0)
    parts = [parts[0]] + [turn(parts[k], twiddles[0, k:k + 1], -twiddles[1, k:k + 1]) for k in range(1, radix)]
    stacked = jnp.concatenate([jnp.concatenate(part, axis=1) for part in parts], axis=0)
    spectra = times_table(stacked, table)
    return [(spectra[k * rows:(k + 1) * rows, :short], spectra[k * rows:(k + 1) * rows, short:]) for k in range(radix)]


def rows_inverse(parts, table, twiddles):
    rows, short = parts[0][0].shape
    stacked = jnp.concatenate([jnp.concatenate(part, axis=1) for part in parts], axis=0)
    fields = times_table(stacked, table)
    parts = [(fields[k * rows:(k + 1) * rows, :short], fields[k * rows:(k + 1) * rows, short:]) for k in range(radix)]
    parts = [parts[0]] + [turn(parts[k], twiddles[0, k:k + 1], twiddles[1, k:k + 1]) for k in range(1, radix)]
    return butterfly(parts, 1.0)


def small_sincos(angle):
    square = angle * angle
    sine = 1.0
    for n in (14, 12, 10, 8, 6, 4, 2):
        sine = 1.0 - square * (1.0 / (n * (n + 1))) * sine
    cosine = 1.0
    for n in (13, 11, 9, 7, 5, 3, 1):
        cosine = 1.0 - square * (1.0 / (n * (n + 1))) * cosine
    return angle * sine, cosine


def spread_kernel(axes, x_total, y_total, step_rows, fields_ref, slow_ref, scalars_ref, out_ref, slow_out, prop_ref,
                  send_sem, recv_sem, self_sem, near_send, near_recv, far_send, far_recv, slow_sem):
    gy, fld, freq_devs, shots = axes
    x, shot = lax.axis_index("freq"), lax.axis_index("shot")
    share = slow_out.shape[3]
    my_share = shot * freq_devs + x
    me, core = lax.axis_index("gy"), lax.axis_index("fld")
    freqs = fields_ref.shape[2]
    half = out_ref.shape[2]
    barrier = pltpu.get_barrier_semaphore()
    for dz in range(gy):
        for dc in range(fld):
            if dz + dc > 0:
                pl.semaphore_signal(
                    barrier, inc=1, device_id_type=MESH,
                    device_id={"gy": lax.rem(me + dz, gy), "fld": lax.rem(core + dc, fld)},
                )
    others = [(ds, dx) for ds in range(shots) for dx in range(freq_devs) if ds + dx > 0]

    def peer(ds, dx):
        return {"shot": lax.rem(shot + ds, shots), "freq": lax.rem(x + dx, freq_devs)}

    for ds, dx in others:
        pl.semaphore_signal(barrier, inc=1, device_id_type=MESH, device_id=peer(ds, dx))
    pl.semaphore_wait(barrier, gy * fld - 1 + len(others))

    def near(dz):
        rows = pl.ds(pl.multiple_of(core * half + my_share * share, share), share)
        return pltpu.make_async_remote_copy(
            src_ref=slow_ref.at[:, rows, :], dst_ref=slow_out.at[me, my_share],
            send_sem=near_send.at[dz - 1], recv_sem=near_recv.at[dz - 1],
            device_id={"gy": lax.rem(me + dz, gy)}, device_id_type=MESH,
        )

    def far(dz, n):
        piece = slow_out.at[lax.rem(me - dz + gy, gy), my_share]
        return pltpu.make_async_remote_copy(
            src_ref=piece, dst_ref=piece, send_sem=far_send.at[dz - 1, n], recv_sem=far_recv.at[dz - 1, n],
            device_id=peer(*others[n]), device_id_type=MESH,
        )

    def near_wait(dz):
        piece = slow_out.at[lax.rem(me - dz + gy, gy), my_share]
        pltpu.make_async_remote_copy(
            src_ref=piece, dst_ref=piece, send_sem=near_send.at[dz - 1], recv_sem=near_recv.at[dz - 1],
            device_id={"gy": lax.rem(me + dz, gy)}, device_id_type=MESH,
        ).wait_recv()

    def far_wait(dz, n):
        ds, dx = others[n]
        share_of = lax.rem(shot - ds + shots, shots) * freq_devs + lax.rem(x - dx + freq_devs, freq_devs)
        piece = slow_out.at[lax.rem(me - dz + gy, gy), share_of]
        pltpu.make_async_remote_copy(
            src_ref=piece, dst_ref=piece, send_sem=far_send.at[dz - 1, n], recv_sem=far_recv.at[dz - 1, n],
            device_id=peer(ds, dx), device_id_type=MESH,
        ).wait_recv()

    local = [
        pltpu.make_async_copy(
            slow_ref.at[:, pl.ds(pl.multiple_of(core * half + q * share, share), share), :],
            slow_out.at[me, q], slow_sem.at[q],
        )
        for q in range(freq_devs * shots)
    ]
    for dz in range(1, gy):
        near(dz).start()

    def remote(f, h):
        return pltpu.make_async_remote_copy(
            src_ref=fields_ref.at[0, :, f, pl.ds(h * half, half), :],
            dst_ref=out_ref.at[me],
            send_sem=send_sem.at[f * fld + h],
            recv_sem=recv_sem.at[me],
            device_id={"gy": f * fld + core, "fld": h},
            device_id_type=MESH,
        )

    own_f, own_h = me // fld, core
    is_mine = lax.rem(me, fld) == core
    own = pltpu.make_async_copy(
        fields_ref.at[0, :, own_f, pl.ds(pl.multiple_of(own_h * half, half), half), :], out_ref.at[me], self_sem
    )
    order = [(f, h) for f in range(freqs) for h in range(fld)]
    for f, h in order:
        mine = jnp.logical_and(f * fld + core == me, core == h)

        @pl.when(jnp.logical_not(mine))
        def _(f=f, h=h):
            remote(f, h).start()

    @pl.when(is_mine)
    def _():
        own.start()

    for copy in local:
        copy.start()

    omega, polarity = scalars_ref[0], scalars_ref[1]
    x_short, y_short = x_total // radix, y_total // radix
    width = prop_ref.shape[2]

    @pl.loop(0, x_total // step_rows)
    def _(step):
        start = pl.multiple_of(step * step_rows, step_rows)
        stored_x = start + lax.broadcasted_iota(jnp.int32, (step_rows, width), 0)
        stored_y = core * width + lax.broadcasted_iota(jnp.int32, (step_rows, width), 1)
        x_index = stored_x // x_short + radix * (stored_x % x_short)
        y_index = stored_y // y_short + radix * (stored_y % y_short)
        lateral = wave_number(x_index, x_total) ** 2 + wave_number(y_index, y_total) ** 2
        kz_square = (omega * reference_slowness) ** 2 - lateral
        kz_root = jnp.sqrt(jnp.abs(kz_square))
        travels = kz_square >= 0.0
        amplitude = jnp.where(travels, 1.0, jnp.exp(-kz_root * depth_interval)) * (1.0 / (x_total * y_total))
        sine, cosine = small_sincos(jnp.where(travels, 0.5 * polarity * kz_root * depth_interval, 0.0))
        prop_ref[0, pl.ds(start, step_rows), :] = amplitude * (1.0 - 2.0 * sine * sine)
        prop_ref[1, pl.ds(start, step_rows), :] = amplitude * (2.0 * sine * cosine)

    for dz in range(1, gy):
        near_wait(dz)
        for n in range(len(others)):
            far(dz, n).start()

    for f, h in order:
        mine = jnp.logical_and(f * fld + core == me, core == h)

        @pl.when(jnp.logical_not(mine))
        def _(f=f, h=h):
            remote(f, h).wait_send()

    for source in range(gy):
        mine = jnp.logical_and(is_mine, me == source)

        @pl.when(jnp.logical_not(mine))
        def _(source=source):
            pltpu.make_async_remote_copy(
                src_ref=out_ref.at[source], dst_ref=out_ref.at[source],
                send_sem=send_sem.at[0], recv_sem=recv_sem.at[source],
                device_id={"gy": me, "fld": 1 - core}, device_id_type=MESH,
            ).wait_recv()

    @pl.when(is_mine)
    def _():
        own.wait()

    for copy in local:
        copy.wait()
    for dz in range(1, gy):
        near(dz).wait_send()
        for n in range(len(others)):
            far_wait(dz, n)
            far(dz, n).wait_send()


def spread(fields, slowness, scalars, axes, x_total, y_total):
    gy, fld, freq_devs, shots = axes
    half = fields.shape[3] // fld
    width = y_total // fld
    return pl.pallas_call(
        functools.partial(spread_kernel, axes, x_total, y_total, 16),
        name="spread",
        out_shape=(
            jax.ShapeDtypeStruct((gy, 2, half, y_total), jnp.float32),
            jax.ShapeDtypeStruct(
                (gy, freq_devs * shots, slowness.shape[0], half // (freq_devs * shots), y_total), jnp.float32
            ),
            jax.ShapeDtypeStruct((2, x_total, width), jnp.float32),
        ),
        in_specs=[pl.BlockSpec(memory_space=pl.ANY), pl.BlockSpec(memory_space=pl.ANY), pl.BlockSpec(memory_space=pltpu.SMEM)],
        out_specs=(
            pl.BlockSpec(memory_space=pl.ANY), pl.BlockSpec(memory_space=pl.ANY), pl.BlockSpec(memory_space=pltpu.VMEM)
        ),
        scratch_shapes=[
            pltpu.SemaphoreType.DMA((fields.shape[2] * fld,)),
            pltpu.SemaphoreType.DMA((gy,)),
            pltpu.SemaphoreType.DMA,
            pltpu.SemaphoreType.DMA((gy - 1,)),
            pltpu.SemaphoreType.DMA((gy - 1,)),
            pltpu.SemaphoreType.DMA((gy - 1, freq_devs * shots - 1)),
            pltpu.SemaphoreType.DMA((gy - 1, freq_devs * shots - 1)),
            pltpu.SemaphoreType.DMA((freq_devs * shots,)),
        ],
        compiler_params=pltpu.CompilerParams(collective_id=0, has_side_effects=True, vmem_limit_bytes=16 * 2**20),
        cost_estimate=pl.CostEstimate(flops=10**8, bytes_accessed=3 * 10**8, transcendentals=10**6),
    )(fields, slowness, scalars)


def write_spectrum(out_ref, spectra):
    per_core = radix // out_ref.shape[0]
    short = spectra[0][0].shape[1]
    for k in range(radix):
        lanes = pl.ds(k % per_core * short, short)
        for part in range(2):
            out_ref[k // per_core, 0, part, :, lanes] = spectra[k][part]


def lane_parts(ref, index, short):
    return [
        tuple(ref[index + (part, slice(None), pl.ds(n * short, short))] for part in range(2)) for n in range(radix)
    ]


def first_kernel(field_ref, table_ref, twiddle_ref, out_ref):
    short = twiddle_ref.shape[2]
    write_spectrum(out_ref, rows_forward(lane_parts(field_ref, (0,), short), table_ref, twiddle_ref[...]))


def middle_kernel(blocks_ref, prop_ref, table_ref, back_ref, twiddle_ref, out_ref):
    cores, chunks, _, short, _ = blocks_ref.shape
    parts = [(blocks_ref[c, n, 0], blocks_ref[c, n, 1]) for n in range(chunks) for c in range(cores)]
    parts = butterfly(parts, -1.0)
    fields = []
    for k in range(radix):
        cosine, sine = twiddle_ref[0, k], twiddle_ref[1, k]
        part = parts[k] if k == 0 else turn(parts[k], cosine, -sine)
        spectrum = table_times(back_ref, jnp.concatenate(part, axis=0))
        rows = slice(k * short, (k + 1) * short)
        part = turn((spectrum[:short], spectrum[short:]), prop_ref[0, rows, :], prop_ref[1, rows, :])
        field = table_times(table_ref, jnp.concatenate(part, axis=0))
        part = (field[:short], field[short:])
        fields.append(part if k == 0 else turn(part, cosine, sine))
    fields = butterfly(fields, 1.0)
    for n in range(chunks):
        for c in range(cores):
            for part in range(2):
                out_ref[c, n, part] = fields[n * cores + c][part]


def last_kernel(more, blocks_ref, slow_ref, scalars_ref, table_ref, back_ref, twiddle_ref, field_ref, *next_ref):
    short = twiddle_ref.shape[2]
    per_core = radix // blocks_ref.shape[0]
    parts = [
        tuple(blocks_ref[k // per_core, 0, part, :, pl.ds(k % per_core * short, short)] for part in range(2))
        for k in range(radix)
    ]
    parts = rows_inverse(parts, back_ref, twiddle_ref[...])
    omega, polarity = scalars_ref[0], scalars_ref[1]
    turned = []
    for n in range(radix):
        lanes = slice(n * short, (n + 1) * short)
        slow = jnp.concatenate([slow_ref[0, q, 0, :, lanes] for q in range(slow_ref.shape[1])], axis=0)
        sine, cosine = small_sincos(polarity * omega * ((slow - reference_slowness) * depth_interval))
        part = turn(parts[n], cosine, sine)
        for side in range(2):
            field_ref[0, side, :, lanes] = part[side]
        turned.append(part)
    if more:
        write_spectrum(next_ref[0], rows_forward(turned, table_ref, twiddle_ref[...]))


def one_field_per_chip(wavefields, slowness, freq_index):
    x_rows, y_total = wavefields.shape[3:]
    gy, fld = lax.axis_size("gy"), lax.axis_size("fld")
    freq_devs, shots = lax.axis_size("freq"), lax.axis_size("shot")
    x_total = x_rows * gy
    half, width = x_rows // fld, y_total // fld
    short = y_total // radix
    z, x = lax.axis_index("gy"), lax.axis_index("freq")
    omega = omega_unit * lax.dynamic_index_in_dim(freq_index, z // fld, keepdims=False).astype(jnp.float32)
    polarity = (2 * (z % fld) - 1).astype(jnp.float32)
    scalars = jnp.stack([omega, polarity])

    table, back = (jnp.asarray(t) for t in split_table(short))
    angles = twiddle_angles(y_total)
    lane_twiddle = jnp.asarray(np.stack([np.cos(angles), np.sin(angles)]).astype(np.float32))
    cols = min(256, width)
    row_twiddle = jnp.broadcast_to(lane_twiddle[..., None], (2, radix, short, cols))

    share = half // (freq_devs * shots)
    field, slow, prop = spread(wavefields, slowness, scalars, (gy, fld, freq_devs, shots), x_total, y_total)

    smem = pl.BlockSpec(memory_space=pltpu.SMEM)
    whole = pl.BlockSpec((2, 2 * short, 2 * short), lambda i: (0, 0, 0))
    lane_tw = pl.BlockSpec((2, radix, short), lambda i: (0, 0, 0))
    field_spec = pl.BlockSpec((1, 2, half, y_total), lambda i: (i, 0, 0, 0))
    spec_spec = pl.BlockSpec((fld, 1, 2, half, width), lambda i: (0, i, 0, 0, 0))
    spec_shape = jax.ShapeDtypeStruct((fld, gy, 2, half, width), jnp.float32)
    field_shape = jax.ShapeDtypeStruct((gy, 2, half, y_total), jnp.float32)
    col_spec = pl.BlockSpec((fld, gy, 2, half, cols), lambda i: (0, 0, 0, 0, i))
    params = pltpu.CompilerParams(vmem_limit_bytes=40 * 2**20)
    cost = pl.CostEstimate(flops=12 * 2 * 2 * short * x_total * y_total // fld, bytes_accessed=12 * x_total * y_total, transcendentals=0)

    spectrum = pl.pallas_call(
        first_kernel, name="first", grid=(gy,), out_shape=spec_shape,
        in_specs=[field_spec, whole, lane_tw], out_specs=spec_spec, compiler_params=params, cost_estimate=cost,
    )(field, table, lane_twiddle)

    images = []
    for depth_step in range(DEPTH):
        more = depth_step + 1 < DEPTH
        blocks = lax.all_to_all(spectrum, "fld", split_axis=0, concat_axis=0, tiled=True)
        middle = pl.pallas_call(
            middle_kernel, name="middle", grid=(width // cols,), out_shape=spec_shape,
            in_specs=[
                col_spec, pl.BlockSpec((2, x_total, cols), lambda i: (0, 0, i)), whole, whole,
                pl.BlockSpec((2, radix, short, cols), lambda i: (0, 0, 0, 0)),
            ],
            out_specs=col_spec, compiler_params=params, cost_estimate=cost,
        )
        blocks = middle(blocks, prop, table, back, row_twiddle)
        blocks = lax.all_to_all(blocks, "fld", split_axis=0, concat_axis=0, tiled=True)
        slow_spec = pl.BlockSpec(
            (1, freq_devs * shots, 1, share, y_total), lambda i, d=depth_step: (i, 0, d, 0, 0)
        )
        out = pl.pallas_call(
            functools.partial(last_kernel, more), name="last", grid=(gy,),
            out_shape=(field_shape, spec_shape) if more else (field_shape,),
            in_specs=[spec_spec, slow_spec, smem, whole, whole, lane_tw],
            out_specs=(field_spec, spec_spec) if more else (field_spec,), compiler_params=params, cost_estimate=cost,
        )(blocks, slow, scalars, table, back, lane_twiddle)
        if more:
            spectrum = out[1]
        images.append(image_of(out[0], z, x, gy, fld, freq_devs))
    return jnp.stack(images)


def image_of(field, z, x, gy, fld, freq_devs):
    _, _, _, y_total = field.shape
    side, group = z % fld, z // fld
    core = lax.axis_index("fld")
    width = y_total // freq_devs

    def block(i, side):
        return lax.dynamic_index_in_dim(field, i * fld + side, axis=0, keepdims=False)

    def swapped(i, after=None):
        sent = block(i, 1 - side)
        other = lax.ppermute(sent, "gy", [(i, i ^ 1) for i in range(gy)])
        if after is not None:
            other, _ = lax.optimization_barrier((other, after))
        term = jnp.sum(block(i, side) * other, axis=0)
        sent = lax.dynamic_slice_in_dim(term, (1 - x) * width, width, axis=1)
        kept = lax.dynamic_slice_in_dim(term, x * width, width, axis=1)
        return kept + lax.ppermute(sent, "freq", [(0, 1), (1, 0)])

    leaving = swapped(1 - group)
    arrived = lax.ppermute(leaving, "gy", [(i, i ^ 2) for i in range(gy)])
    staying = swapped(group, leaving)
    rows = staying + arrived
    width = width // fld
    sent = lax.dynamic_slice_in_dim(rows, (1 - core) * width, width, axis=1)
    kept = lax.dynamic_slice_in_dim(rows, core * width, width, axis=1)
    other = lax.ppermute(sent, "fld", [(0, 1), (1, 0)])
    first = core == 0
    return jnp.concatenate([jnp.where(first, kept, other), jnp.where(first, other, kept)], axis=0)


def fits(mesh, wavefields):
    shape = dict(mesh.shape)
    freqs = wavefields.shape[2] // (shape["shot"] * shape["freq"])
    x_total, y_total = wavefields.shape[3:]
    return (
        shape["gy"] == 4 == freqs * shape["fld"] and shape["fld"] == 2 and shape["freq"] == 2
        and x_total == y_total and y_total % (radix * 128) == 0
        and x_total // shape["gy"] // shape["fld"] % (8 * shape["freq"] * shape["shot"]) == 0
    )


def solution(mesh):
    placed = (P("fld", None, ("shot", "freq"), "gy", None), P(None, "gy", None), P("freq"))

    def run(wavefields, slowness, freq_index):
        engaged = fits(mesh, wavefields)
        step = jax.shard_map(
            one_field_per_chip if engaged else per_device,
            mesh=mesh,
            in_specs=placed,
            out_specs=P("shot", "gy", ("freq", "fld")),
            check_vma=False,
        )
        return step(wavefields, slowness, freq_index)

    return run
```
